256 devices in a mesh: dp: 8 (over y, core), space: 32 (over z, x).
Axes of the slice: x: 4, y: 4, z: 8, core: 2. Of those that a mesh axis runs over, the one named last changes fastest.
Arguments:
- features: bfloat16 [8, 64, 64, 256], P('dp', None, 'space'), may hold values from -6 to 6
- kernel_a: bfloat16 [27, 64, 128], replicated, may hold values from -0.15625 to 0.15625
- kernel_b: bfloat16 [27, 128, 256], replicated, may hold values from -0.109375 to 0.109375
- upstream: bfloat16 [8, 256, 32, 64], P('dp', None, 'space'), may hold values from -24 to 24
Outputs:
- grad_input: bfloat16 [8, 64, 64, 256], P('dp', None, 'space')
- grad_kernel_a: float32 [27, 64, 128], replicated
- grad_kernel_b: float32 [27, 128, 256], P(None, None, 'space')
The draws below stay inside these ranges and needn't reach their ends.
All inputs are finite; a program needn't handle non-finite values.
Results may differ from the reference program's by a relative error of at most 0.0075.
Values may be sent and summed in bfloat16 or wider, within the bound.
A program may use at most 64 MiB of HBM per device.

```python
import math
import jax
import jax.numpy as jnp
from jax import lax

CIN_A = 64
COUT_A = 128
COUT_B = 256
GY = 16
GZ = 16
SAMPLES = 8
GX = 64


def level_of(key, dims, split, least, high):
    gain = 1.0
    for position, shards_of in split:
        steps = jax.random.uniform(jax.random.fold_in(jax.random.fold_in(key, 6), position), (shards_of,), jnp.float32, least / len(split), high / len(split))
        gain = gain * jnp.repeat(jnp.exp(steps), dims[position] // shards_of).reshape((-1,) + (1,) * (len(dims) - 1 - position))
    return gain


def bell_draw(key, dims, scale, limit, cuts=(), held_as=jnp.bfloat16):
    factor_of = level_of(key, dims, cuts, -0.22, 0.18) if cuts else 1.0
    values = jax.random.normal(key, dims, jnp.float32) * scale * factor_of
    return jnp.minimum(jnp.maximum(values, -limit), limit).astype(held_as)


def setup_inputs(seed: int = 0) -> dict:
    seeds = jax.random.split(jax.random.key(seed), 5)
    return {
        "features": bell_draw(seeds[0], (SAMPLES, CIN_A, GX, GY * GZ), 1.0, 6.0, ((0, 8), (2, 32))),
        "kernel_a": bell_draw(seeds[1], (27, CIN_A, COUT_A), (27 * CIN_A) ** -0.5, 0.15625),
        "kernel_b": bell_draw(seeds[2], (27, COUT_A, COUT_B), (27 * COUT_A) ** -0.5, 0.109375),
        "upstream": bell_draw(seeds[3], (SAMPLES, COUT_B, GX // 2, GY * GZ // 4), 4.0, 24.0, ((0, 8), (2, 32))),
    }


def conv_forward(source, kernel):
    channels = source.shape[0]
    size_x, size_y, size_z = (source.shape[1], source.shape[2], source.shape[3])
    padded = jnp.pad(source, ((0, 0), (1, 1), (1, 1), (1, 1)))
    summed = jnp.zeros((kernel.shape[2], size_x * size_y * size_z), jnp.float32)
    for tap_index in range(27):
        along_x, along_y, along_z = (tap_index // 9, tap_index // 3 % 3, tap_index % 3)
        shifted = padded[:, along_x:along_x + size_x, along_y:along_y + size_y, along_z:along_z + size_z].reshape(channels, -1)
        summed = summed + jnp.dot(kernel[tap_index].T, shifted, preferred_element_type=jnp.float32)
    return summed.reshape(-1, size_x, size_y, size_z)

def conv_transposed(gradient, kernel):
    channels = gradient.shape[0]
    size_x, size_y, size_z = (gradient.shape[1], gradient.shape[2], gradient.shape[3])
    padded = jnp.pad(gradient, ((0, 0), (1, 1), (1, 1), (1, 1)))
    summed = jnp.zeros((kernel.shape[1], size_x * size_y * size_z), jnp.float32)
    for tap_index in range(27):
        along_x, along_y, along_z = (2 - tap_index // 9, 2 - tap_index // 3 % 3, 2 - tap_index % 3)
        shifted = padded[:, along_x:along_x + size_x, along_y:along_y + size_y, along_z:along_z + size_z].reshape(channels, -1)
        summed = summed + jnp.dot(kernel[tap_index], shifted, preferred_element_type=jnp.float32)
    return summed.reshape(-1, size_x, size_y, size_z)

def kernel_grad(source, gradient):
    channels = source.shape[0]
    size_x, size_y, size_z = (source.shape[1], source.shape[2], source.shape[3])
    padded = jnp.pad(source, ((0, 0), (1, 1), (1, 1), (1, 1)))
    flat_grad = gradient.reshape(gradient.shape[0], -1)
    terms = []
    for tap_index in range(27):
        along_x, along_y, along_z = (tap_index // 9, tap_index // 3 % 3, tap_index % 3)
        shifted = padded[:, along_x:along_x + size_x, along_y:along_y + size_y, along_z:along_z + size_z].reshape(channels, -1)
        terms.append(jnp.dot(shifted, flat_grad.T, preferred_element_type=jnp.float32))
    return jnp.stack(terms)

def silu_slope(value):
    sigma = jax.nn.sigmoid(value)
    return sigma * (1.0 + value * (1.0 - sigma))

def reference(features, kernel_a, kernel_b, upstream):

    def one_sample(running, sample_items):
        field, upstream_one = sample_items
        source = field.reshape(CIN_A, GX, GY, GZ)
        pre_a = conv_forward(source, kernel_a)
        pooled = jax.nn.silu(pre_a).reshape(COUT_A, GX // 2, 2, GY // 2, 2, GZ // 2, 2).mean(axis=(2, 4, 6)).astype(jnp.bfloat16)
        pre_b = conv_forward(pooled, kernel_b)
        upstream_grid = upstream_one.reshape(COUT_B, GX // 2, GY // 2, GZ // 2).astype(jnp.float32)
        grad_pre_b = (upstream_grid * silu_slope(pre_b)).astype(jnp.bfloat16)
        term_b = kernel_grad(pooled, grad_pre_b)
        grad_pool = conv_transposed(grad_pre_b, kernel_b)
        spread = jnp.broadcast_to(grad_pool.reshape(COUT_A, GX // 2, 1, GY // 2, 1, GZ // 2, 1), (COUT_A, GX // 2, 2, GY // 2, 2, GZ // 2, 2)).reshape(COUT_A, GX, GY, GZ)
        grad_pre_a = (spread * 0.125 * silu_slope(pre_a)).astype(jnp.bfloat16)
        term_a = kernel_grad(source, grad_pre_a)
        grad_in = conv_transposed(grad_pre_a, kernel_a).astype(jnp.bfloat16).reshape(CIN_A, GX, GY * GZ)
        return ((running[0] + term_a, running[1] + term_b), grad_in)
    start = (jnp.zeros((27, CIN_A, COUT_A), jnp.float32), jnp.zeros((27, COUT_A, COUT_B), jnp.float32))
    totals, grad_input = lax.scan(one_sample, start, (features, upstream))
    scale_a = 1.0 / math.sqrt(SAMPLES * GX * GY * GZ)
    scale_b = 1.0 / math.sqrt(SAMPLES * GX * GY * GZ / 8)
    return (grad_input, totals[0] * scale_a, totals[1] * scale_b)
```

```python
import functools
import math

import jax
import jax.numpy as jnp
from jax import lax
from jax.experimental import pallas as pl
from jax.experimental.pallas import tpu as pltpu
from jax.sharding import PartitionSpec as P

GY = 16
GZ = 16
CELLS = GY * GZ
HY = GY // 2
HZ = GZ // 2
POOL = HY * HZ
MESH = pl.DeviceIdType.MESH
F32 = jnp.float32
BF16 = jnp.bfloat16

X_R, X_L, P_R, P_L, G_R, G_L, A_R, A_L, DP_P, DP_G, A1, A2, A3, A4, B2, B3, N_SEM = range(17)


def sigmoid(value):
    return 1.0 / (1.0 + jnp.exp(-value))


def slope(value, sigma):
    return sigma * (1.0 + value * (1.0 - sigma))


def shift_column(value, step, span):
    if step == 0:
        return value
    rows = value.shape[0]
    column = lax.broadcasted_iota(jnp.int32, value.shape, 0) % span + step
    moved = pltpu.roll(value, (-step) % rows, 0)
    return jnp.where((column >= 0) & (column < span), moved, 0.0)


def shift_block(value, step):
    if step == 0:
        return value
    zeros = jnp.zeros((abs(step), value.shape[1]), value.dtype)
    if step > 0:
        return jnp.concatenate([value[step:], zeros], axis=0)
    return jnp.concatenate([zeros, value[:step]], axis=0)


def kernel(
    nd, ns, scale_a, scale_b,
    x_ref, wa_ref, wb_ref, up_ref,
    gi_ref, ga_ref, gb_ref,
    xh, xz, slope_a, act_a, pown, ph, gbown, gbh, gaown, gah, gz, kr, spread,
    psend, precv, grecv, pcol, a1send, a1recv, a2send, a2recv, a3buf, a4buf,
    bsend, brecv, bag, send, recv,
):
    s = lax.axis_index("space")
    d = lax.axis_index("dp")
    right = lax.rem(s + 1, ns)
    left = lax.rem(s + ns - 1, ns)
    has_left = s > 0
    has_right = s < ns - 1

    barrier = pltpu.get_barrier_semaphore()

    def greet_space(k, c):
        pl.semaphore_signal(barrier, inc=1, device_id={"space": lax.rem(s + k, ns)}, device_id_type=MESH)
        return c

    def greet_dp(k, c):
        pl.semaphore_signal(barrier, inc=1, device_id={"dp": lax.rem(d + k, nd)}, device_id_type=MESH)
        return c

    lax.fori_loop(1, ns, greet_space, 0)
    lax.fori_loop(1, nd, greet_dp, 0)

    for t in range(9):
        for j in range(3):
            kr[t, :, j * 128 : (j + 1) * 128] = wa_ref[t, j * 64 : (j + 1) * 64, :]
    for q in range(4):
        xz[q, 0:GZ, :] = jnp.zeros((GZ, 192), BF16)
        xz[q, GZ + CELLS : 2 * GZ + CELLS, :] = jnp.zeros((GZ, 192), BF16)
        gz[q, 0:GZ, :] = jnp.zeros((GZ, 384), BF16)
        gz[q, GZ + CELLS : 2 * GZ + CELLS, :] = jnp.zeros((GZ, 384), BF16)

    pl.semaphore_wait(barrier, ns + nd - 2)

    def remote(src, dst, slot, device):
        return pltpu.make_async_remote_copy(
            src_ref=src, dst_ref=dst, send_sem=send.at[slot], recv_sem=recv.at[slot],
            device_id=device, device_id_type=MESH,
        )

    def halo(lower, upper, landing, slot_r, slot_l):
        to_right = remote(upper, landing.at[0], slot_r, {"space": right})
        to_left = remote(lower, landing.at[1], slot_l, {"space": left})
        to_right.start()
        to_left.start()
        return to_right, to_left

    def to_all(axis, me, count, src_of, dst, slot):
        def step(k, c):
            other = lax.rem(me + k, count)
            remote(src_of(other), dst.at[me], slot, {axis: other}).start()
            return c

        lax.fori_loop(1, count, step, 0)

    def wait_all(sems, slot, buf, count):
        part = buf.at[pl.ds(0, count - 1)]
        pltpu.make_async_copy(part, part, sems.at[slot]).wait()

    x_halo = halo(x_ref.at[0], x_ref.at[1], xh, X_R, X_L)

    def put_xz(q, plane):
        rows = plane.astype(F32).T
        wide = jnp.concatenate([shift_column(rows, -1, GZ), rows, shift_column(rows, 1, GZ)], axis=1)
        xz[q, GZ : GZ + CELLS, :] = wide.astype(BF16)

    put_xz(1, x_ref[0])
    put_xz(2, x_ref[1])

    def conv_a_terms(q, exs):
        total = None
        for ex in exs:
            for ey in range(3):
                part = jnp.dot(
                    xz[q + ex, ey * GZ : ey * GZ + CELLS, :], wa_ref[ex * 3 + ey],
                    preferred_element_type=F32,
                )
                total = part if total is None else total + part
        return total

    act_a[0:CELLS, :] = conv_a_terms(0, (1, 2))
    act_a[CELLS : 2 * CELLS, :] = conv_a_terms(1, (0, 1))
    x_halo[0].wait_recv()
    put_xz(0, jnp.where(has_left, xh[0].astype(F32), 0.0))
    x_halo[1].wait_recv()
    put_xz(3, jnp.where(has_right, xh[1].astype(F32), 0.0))
    for q in range(2):
        area = slice(q * CELLS, (q + 1) * CELLS)
        pre = act_a[area, :] + conv_a_terms(q, (0,) if q == 0 else (2,))
        sigma = sigmoid(pre)
        act_a[area, :] = pre * sigma
        slope_a[area, :] = slope(pre, sigma) * 0.125

    pairs = act_a[pl.ds(0, CELLS, stride=2), :] + act_a[pl.ds(1, CELLS, stride=2), :]
    pairs = pairs.reshape(2, HY, 2, HZ, 128)
    pooled = (pairs[0, :, 0] + pairs[0, :, 1] + pairs[1, :, 0] + pairs[1, :, 1]).reshape(POOL, 128) * 0.125
    pown[...] = pooled.astype(BF16)
    p_halo = halo(pown, pown, ph, P_R, P_L)

    def conv_b_terms(plane, ex):
        taps = []
        moved = [shift_column(plane, step, HZ) for step in (-1, 0, 1)]
        for ey in range(3):
            for ez in range(3):
                taps.append(shift_block(moved[ez], (ey - 1) * HZ).astype(BF16))
        return jnp.dot(jnp.concatenate(taps, axis=1), wb_ref[ex], preferred_element_type=F32)

    own_p = pown[...].astype(F32)
    pre_b = conv_b_terms(own_p, 1)
    p_halo[0].wait_recv()
    left_p = jnp.where(has_left, ph[0].astype(F32), 0.0)
    pre_b = pre_b + conv_b_terms(left_p, 0)
    p_halo[1].wait_recv()
    right_p = jnp.where(has_right, ph[1].astype(F32), 0.0)
    pre_b = pre_b + conv_b_terms(right_p, 2)
    grad_b = up_ref[...].astype(F32) * slope(pre_b, sigmoid(pre_b))
    gbown[...] = grad_b.astype(BF16)
    g_halo = halo(gbown, gbown, gbh, G_R, G_L)

    chans = 128 // nd
    for e, plane in enumerate((left_p, own_p, right_p)):
        psend[:, e] = plane.T.reshape(nd, chans, POOL).astype(BF16)
    grecv[d] = gbown[...]
    precv[d] = psend[d]
    to_all("dp", d, nd, lambda other: psend.at[other], precv, DP_P)
    to_all("dp", d, nd, lambda other: gbown, grecv, DP_G)

    def conv_bt_terms(plane, ex, total):
        moved = [shift_column(plane, -step, HZ) for step in (-1, 0, 1)]
        for ey in range(3):
            for ez in range(3):
                tap = ey * 3 + ez
                shifted = shift_block(moved[ez], -(ey - 1) * HZ).astype(BF16)
                part = lax.dot_general(
                    shifted, wb_ref[ex, tap * 128 : (tap + 1) * 128, :],
                    (((1,), (1,)), ((), ())), preferred_element_type=F32,
                )
                total = part if total is None else total + part
        return total

    grad_pool = conv_bt_terms(gbown[...].astype(F32), 1, None)
    g_halo[0].wait_recv()
    grad_pool = conv_bt_terms(jnp.where(has_left, gbh[0].astype(F32), 0.0), 2, grad_pool)
    g_halo[1].wait_recv()
    grad_pool = conv_bt_terms(jnp.where(has_right, gbh[1].astype(F32), 0.0), 0, grad_pool)

    tall = jnp.broadcast_to(grad_pool.reshape(HY, 1, HZ, 128), (HY, 2, HZ, 128)).reshape(GY * HZ, 128)
    spread[pl.ds(0, GY * HZ, stride=2), :] = tall
    spread[pl.ds(1, GY * HZ, stride=2), :] = tall
    for q in range(2):
        gaown[q] = (spread[...] * slope_a[q * CELLS : (q + 1) * CELLS, :]).astype(BF16)
    a_halo = halo(gaown.at[0], gaown.at[1], gah, A_R, A_L)

    rows_a = 64 // nd
    grads = [gaown[0], gaown[1]]
    for ex in range(3):
        for ey in range(3):
            term = None
            for q in range(2):
                part = lax.dot_general(
                    xz[q + ex, ey * GZ : ey * GZ + CELLS, :], grads[q],
                    (((0,), (0,)), ((), ())), preferred_element_type=F32,
                )
                term = part if term is None else term + part
            for ez in range(3):
                tap = ex * 9 + ey * 3 + ez
                a1send[:, tap] = term[ez * 64 : (ez + 1) * 64, :].reshape(nd, rows_a, 128).astype(BF16)
    taps_own = a2recv.shape[1]
    for tap in range(27, taps_own * ns):
        a1send[:, tap] = jnp.zeros((nd, rows_a, 128), BF16)
    a1recv[d] = a1send[d]
    to_all("dp", d, nd, lambda other: a1send.at[other], a1recv, A1)

    def put_gz(q, plane):
        wide = jnp.concatenate([shift_column(plane, 1, GZ), plane, shift_column(plane, -1, GZ)], axis=1)
        gz[q, GZ : GZ + CELLS, :] = wide.astype(BF16)

    put_gz(1, gaown[0].astype(F32))
    put_gz(2, gaown[1].astype(F32))
    a_halo[0].wait_recv()
    put_gz(0, jnp.where(has_left, gah[0].astype(F32), 0.0))
    a_halo[1].wait_recv()
    put_gz(3, jnp.where(has_right, gah[1].astype(F32), 0.0))
    for q in range(2):
        total = None
        for ex in range(3):
            for ey in range(3):
                part = lax.dot_general(
                    kr[ex * 3 + ey], gz[q + 2 - ex, (2 - ey) * GZ : (2 - ey) * GZ + CELLS, :],
                    (((1,), (1,)), ((), ())), preferred_element_type=F32,
                )
                total = part if total is None else total + part
        gi_ref[q] = total.astype(BF16)

    wait_all(recv, DP_P, precv, nd)
    wait_all(recv, DP_G, grecv, nd)
    wide_cells = nd * POOL
    lane = lax.broadcasted_iota(jnp.int32, (chans, wide_cells), 1)
    row = lane // HZ % HY
    column = lane % HZ
    for ex in range(3):
        flat = jnp.concatenate([precv[n, ex].astype(F32) for n in range(nd)], axis=1)
        for ey in range(3):
            for ez in range(3):
                step = (ey - 1) * HZ + ez - 1
                inside = (row + ey - 1 >= 0) & (row + ey - 1 < HY) & (column + ez - 1 >= 0) & (column + ez - 1 < HZ)
                moved = flat if step == 0 else pltpu.roll(flat, (-step) % wide_cells, 1)
                tap = ex * 9 + ey * 3 + ez
                pcol[tap * chans : (tap + 1) * chans, :] = jnp.where(inside, moved, 0.0).astype(BF16)
    used = 27 * chans
    padded = pcol.shape[0]
    pcol[used:padded, :] = jnp.zeros((padded - used, wide_cells), BF16)
    part_b = jnp.dot(pcol[...], grecv[...].reshape(wide_cells, 256), preferred_element_type=F32)
    bsend[...] = part_b.T.reshape(ns, 256 // ns, padded).astype(BF16)
    brecv[s] = bsend[s]
    to_all("space", s, ns, lambda other: bsend.at[other], brecv, B2)

    wait_all(recv, A1, a1recv, nd)
    total = a1recv[0].astype(F32)
    for n in range(1, nd):
        total = total + a1recv[n].astype(F32)
    a2send[...] = total.astype(BF16).reshape(a2send.shape)
    a2recv[s] = a2send[s]
    to_all("space", s, ns, lambda other: a2send.at[other], a2recv, A2)

    wait_all(recv, B2, brecv, ns)
    total_b = jnp.sum(brecv[...].astype(F32), axis=0) * scale_b
    bag[d] = total_b.astype(BF16)
    to_all("dp", d, nd, lambda other: bag.at[d], bag, B3)

    wait_all(recv, A2, a2recv, ns)
    total_a = jnp.sum(a2recv[...].astype(F32), axis=0) * scale_a
    a3buf[s] = total_a.astype(BF16)
    to_all("space", s, ns, lambda other: a3buf.at[s], a3buf, A3)
    wait_all(recv, A3, a3buf, ns)
    a4buf[d] = a3buf[...]
    to_all("dp", d, nd, lambda other: a3buf, a4buf, A4)
    wait_all(recv, B3, bag, nd)
    gb_ref[...] = bag[...]
    wait_all(recv, A4, a4buf, nd)
    ga_ref[...] = a4buf[...]

    for pair in (x_halo, p_halo, g_halo, a_halo):
        pair[0].wait_send()
        pair[1].wait_send()
    for slot, buf, count in (
        (DP_P, precv, nd), (DP_G, grecv, nd), (A1, a1recv, nd), (A2, a2recv, ns),
        (A3, a3buf, ns), (A4, a4buf, nd), (B2, brecv, ns), (B3, bag, nd),
    ):
        wait_all(send, slot, buf, count)


def body(nd, ns, scale_a, scale_b, features, kernel_a, kernel_b, upstream):
    x = jnp.transpose(features[0], (1, 0, 2))
    wa = kernel_a.reshape(9, 192, 128)
    wb = kernel_b.reshape(3, 9 * 128, 256)
    up = upstream[0, :, 0, :].T
    rows_a = 64 // nd
    chans = 128 // nd
    taps_own = -(-27 // ns)
    padded = -(-27 * chans // 128) * 128
    vmem = pl.BlockSpec(memory_space=pltpu.VMEM)
    gi, ga, gb = pl.pallas_call(
        functools.partial(kernel, nd, ns, scale_a, scale_b),
        out_shape=(
            jax.ShapeDtypeStruct((2, 64, CELLS), BF16),
            jax.ShapeDtypeStruct((nd, ns, taps_own, rows_a, 128), BF16),
            jax.ShapeDtypeStruct((nd, 256 // ns, padded), BF16),
        ),
        in_specs=[vmem] * 4,
        out_specs=(vmem, vmem, vmem),
        scratch_shapes=[
            pltpu.VMEM((2, 64, CELLS), BF16),
            pltpu.VMEM((4, CELLS + 2 * GZ, 192), BF16),
            pltpu.VMEM((2 * CELLS, 128), F32),
            pltpu.VMEM((2 * CELLS, 128), F32),
            pltpu.VMEM((POOL, 128), BF16),
            pltpu.VMEM((2, POOL, 128), BF16),
            pltpu.VMEM((POOL, 256), BF16),
            pltpu.VMEM((2, POOL, 256), BF16),
            pltpu.VMEM((2, CELLS, 128), BF16),
            pltpu.VMEM((2, CELLS, 128), BF16),
            pltpu.VMEM((4, CELLS + 2 * GZ, 384), BF16),
            pltpu.VMEM((9, 64, 384), BF16),
            pltpu.VMEM((CELLS, 128), F32),
            pltpu.VMEM((nd, 3, chans, POOL), BF16),
            pltpu.VMEM((nd, 3, chans, POOL), BF16),
            pltpu.VMEM((nd, POOL, 256), BF16),
            pltpu.VMEM((padded, nd * POOL), BF16),
            pltpu.VMEM((nd, ns * taps_own, rows_a, 128), BF16),
            pltpu.VMEM((nd, ns * taps_own, rows_a, 128), BF16),
            pltpu.VMEM((ns, taps_own, rows_a, 128), BF16),
            pltpu.VMEM((ns, taps_own, rows_a, 128), BF16),
            pltpu.VMEM((ns, taps_own, rows_a, 128), BF16),
            pltpu.VMEM((nd, ns, taps_own, rows_a, 128), BF16),
            pltpu.VMEM((ns, 256 // ns, padded), BF16),
            pltpu.VMEM((ns, 256 // ns, padded), BF16),
            pltpu.VMEM((nd, 256 // ns, padded), BF16),
            pltpu.SemaphoreType.DMA((N_SEM,)),
            pltpu.SemaphoreType.DMA((N_SEM,)),
        ],
        compiler_params=pltpu.CompilerParams(collective_id=0, has_side_effects=True),
    )(x, wa, wb, up)
    grad_input = jnp.transpose(gi, (1, 0, 2))[None]
    ga = ga.reshape(nd, ns * taps_own, rows_a, 128)[:, :27]
    grad_a = jnp.transpose(ga, (1, 0, 2, 3)).reshape(27, 64, 128).astype(F32)
    gb = gb[:, :, : 27 * chans].reshape(nd, 256 // ns, 27, chans)
    grad_b = jnp.transpose(gb, (2, 0, 3, 1)).reshape(27, 128, 256 // ns).astype(F32)
    return grad_input, grad_a, grad_b


def solution(mesh):
    nd, ns = mesh.shape["dp"], mesh.shape["space"]
    cells_all = nd * 2 * ns * CELLS
    run = functools.partial(body, nd, ns, 1.0 / math.sqrt(cells_all), 1.0 / math.sqrt(cells_all / 8))
    return jax.shard_map(
        run,
        mesh=mesh,
        in_specs=(P("dp", None, "space", None), P(), P(), P("dp", None, "space", None)),
        out_specs=(P("dp", None, "space", None), P(), P(None, None, "space")),
        check_vma=False,
    )
```

```python
import functools
import math

import jax
import jax.numpy as jnp
from jax import lax
from jax.experimental import pallas as pl
from jax.experimental.pallas import tpu as pltpu
from jax.sharding import PartitionSpec as P

GY = 16
GZ = 16
CELLS = GY * GZ
HY = GY // 2
HZ = GZ // 2
POOL = HY * HZ
MESH = pl.DeviceIdType.MESH
F32 = jnp.float32
BF16 = jnp.bfloat16

NC = 2
NX = 4

(
    X_R, X_L, U_R, U_L, P_R, P_L, P_RR, P_LL, A_R, A_L, BP_Y, BG_Y, BP_C, BG_C,
    A_C, A_YX, A_Z, A_OUT, A_OUT_C, B_X, B_Z, B_OUT, N_SEM,
) = range(23)


def sigmoid(value):
    return 1.0 / (1.0 + jnp.exp(-value))


def slope(value, sigma):
    return sigma * (1.0 + value * (1.0 - sigma))


def shift_column(value, step, span):
    if step == 0:
        return value
    rows = value.shape[0]
    column = lax.broadcasted_iota(jnp.int32, value.shape, 0) % span + step
    moved = pltpu.roll(value, (-step) % rows, 0)
    return jnp.where((column >= 0) & (column < span), moved, 0.0)


def shift_block(value, step):
    if step == 0:
        return value
    zeros = jnp.zeros((abs(step), value.shape[1]), value.dtype)
    if step > 0:
        return jnp.concatenate([value[step:], zeros], axis=0)
    return jnp.concatenate([zeros, value[:step]], axis=0)


def kernel(
    nd, ns, scale_a, scale_b,
    x_hbm, wa_hbm, wb_hbm, up_hbm,
    gi_ref, ga_ref, gb_ref,
    x_raw, wa_ref, wb_ref, up_ref, xown, xh, uph, xz, slope_a, act_a, pown, ph, gbown,
    gaown, gah, gz, kr, spread,
    psend, py, pc, gy, gc, pcol, ac_send, ac_recv, ayx_send, ayx_recv, az, aout,
    bx_send, bx_recv, bz_send, bz_recv, bag, load, send, recv,
):
    ny, nz = nd // NC, ns // NX
    s = lax.axis_index("space")
    d = lax.axis_index("dp")
    y, c = d // NC, d % NC
    z, x = s // NX, s % NX
    right = lax.rem(s + 1, ns)
    left = lax.rem(s + ns - 1, ns)
    right2 = lax.rem(s + 2, ns)
    left2 = lax.rem(s + ns - 2, ns)
    has_left = s > 0
    has_right = s < ns - 1
    has_left2 = s > 1
    has_right2 = s < ns - 2
    core = {"dp": y * NC + 1 - c}

    loads = [
        pltpu.make_async_copy(src, dst, load.at[i])
        for i, (src, dst) in enumerate(
            ((x_hbm, x_raw), (up_hbm, up_ref), (wa_hbm, wa_ref), (wb_hbm, wb_ref))
        )
    ]
    for copy in loads:
        copy.start()

    def yx_device(k):
        k_y, k_x = k // NX, k % NX
        return {"dp": lax.rem(y + k_y, ny) * NC + c, "space": z * NX + lax.rem(x + k_x, NX)}

    def z_device(k):
        return {"space": lax.rem(z + k, nz) * NX + x}

    barrier = pltpu.get_barrier_semaphore()

    def greet(device):
        pl.semaphore_signal(barrier, inc=1, device_id=device, device_id_type=MESH)

    for near in (right, left, right2, left2):
        greet({"space": near})

    def greet_yx(k, carry):
        greet(yx_device(k))
        return carry

    def greet_z(k, carry):
        greet(z_device(k))
        return carry

    def greet_dp(k, carry):
        greet({"dp": lax.rem(d + k, nd)})
        return carry

    lax.fori_loop(1, nz, greet_z, 0)
    lax.fori_loop(1, ny * NX, greet_yx, 0)
    lax.fori_loop(1, nd, greet_dp, 0)

    loads[0].wait()
    both = x_raw[...].astype(F32)
    planes = [both[:, 0, :], both[:, 1, :]]
    for q in range(2):
        xown[q] = planes[q].astype(BF16)
    for q in range(4):
        xz[q, 0:GZ, :] = jnp.zeros((GZ, 192), BF16)
        xz[q, GZ + CELLS : 2 * GZ + CELLS, :] = jnp.zeros((GZ, 192), BF16)
        gz[q, 0:GZ, :] = jnp.zeros((GZ, 384), BF16)
        gz[q, GZ + CELLS : 2 * GZ + CELLS, :] = jnp.zeros((GZ, 384), BF16)

    def put_xz(q, plane):
        rows = plane.T
        wide = jnp.concatenate([shift_column(rows, -1, GZ), rows, shift_column(rows, 1, GZ)], axis=1)
        xz[q, GZ : GZ + CELLS, :] = wide.astype(BF16)

    put_xz(1, planes[0])
    put_xz(2, planes[1])
    loads[1].wait()
    loads[2].wait()
    for t in range(9):
        for j in range(3):
            kr[t, :, j * 128 : (j + 1) * 128] = wa_ref[t, j * 64 : (j + 1) * 64, :]

    def conv_a_terms(q, exs):
        total = None
        for ex in exs:
            for ey in range(3):
                part = jnp.dot(
                    xz[q + ex, ey * GZ : ey * GZ + CELLS, :], wa_ref[ex * 3 + ey],
                    preferred_element_type=F32,
                )
                total = part if total is None else total + part
        return total

    pl.semaphore_wait(barrier, 4 + (nz - 1) + (ny * NX - 1) + (nd - 1))

    def remote(src, dst, slot, device):
        return pltpu.make_async_remote_copy(
            src_ref=src, dst_ref=dst, send_sem=send.at[slot], recv_sem=recv.at[slot],
            device_id=device, device_id_type=MESH,
        )

    started = []

    def start(src, dst, slot, device):
        copy = remote(src, dst, slot, device)
        copy.start()
        started.append(copy)
        return copy

    def wait_part(sems, slot, part):
        pltpu.make_async_copy(part, part, sems.at[slot]).wait()

    x_halo = [start(xown.at[1], xh.at[0], X_R, {"space": right}), start(xown.at[0], xh.at[1], X_L, {"space": left})]
    u_halo = [start(up_ref, uph.at[0], U_R, {"space": right}), start(up_ref, uph.at[1], U_L, {"space": left})]

    act_a[0:CELLS, :] = conv_a_terms(0, (1, 2))
    act_a[CELLS : 2 * CELLS, :] = conv_a_terms(1, (0, 1))
    x_halo[0].wait_recv()
    put_xz(0, jnp.where(has_left, xh[0].astype(F32), 0.0))
    x_halo[1].wait_recv()
    put_xz(3, jnp.where(has_right, xh[1].astype(F32), 0.0))
    for q in range(2):
        area = slice(q * CELLS, (q + 1) * CELLS)
        pre = act_a[area, :] + conv_a_terms(q, (0,) if q == 0 else (2,))
        sigma = sigmoid(pre)
        act_a[area, :] = pre * sigma
        slope_a[area, :] = slope(pre, sigma) * 0.125

    pairs = act_a[pl.ds(0, CELLS, stride=2), :] + act_a[pl.ds(1, CELLS, stride=2), :]
    pairs = pairs.reshape(2, HY, 2, HZ, 128)
    pooled = (pairs[0, :, 0] + pairs[0, :, 1] + pairs[1, :, 0] + pairs[1, :, 1]).reshape(POOL, 128) * 0.125
    pown[...] = pooled.astype(BF16)
    p_halo = [
        start(pown, ph.at[0], P_RR, {"space": right2}),
        start(pown, ph.at[3], P_LL, {"space": left2}),
        start(pown, ph.at[1], P_R, {"space": right}),
        start(pown, ph.at[2], P_L, {"space": left}),
    ]

    def taps_of(plane):
        moved = [shift_column(plane, step, HZ) for step in (-1, 0, 1)]
        taps = []
        for ey in range(3):
            for ez in range(3):
                taps.append(shift_block(moved[ez], (ey - 1) * HZ).astype(BF16))
        return jnp.concatenate(taps, axis=1)

    own_p = pown[...].astype(F32)
    own_taps = taps_of(own_p)
    loads[3].wait()
    p_halo[2].wait_recv()
    p_halo[3].wait_recv()
    left_p = jnp.where(has_left, ph[1].astype(F32), 0.0)
    right_p = jnp.where(has_right, ph[2].astype(F32), 0.0)

    chans = 128 // nd
    for e, plane in enumerate((left_p, own_p, right_p)):
        psend[:, :, e] = plane.T.reshape(NC, ny, chans, POOL).astype(BF16)
    for cc in range(NC):
        py[cc, y] = psend[cc, y]

    def p_step(k, carry):
        other = lax.rem(y + k, ny)
        for cc in range(NC):
            remote(psend.at[cc, other], py.at[cc, y], BP_Y, {"dp": other * NC + c}).start()
        return carry

    lax.fori_loop(1, ny, p_step, 0)
    left_taps = taps_of(left_p)
    right_taps = taps_of(right_p)
    p_halo[0].wait_recv()
    p_halo[1].wait_recv()
    left2_taps = taps_of(jnp.where(has_left2, ph[0].astype(F32), 0.0))
    right2_taps = taps_of(jnp.where(has_right2, ph[3].astype(F32), 0.0))
    order = (left2_taps, left_taps, own_taps, right_taps, right2_taps)
    pre_b = None
    for ex in range(3):
        part = jnp.dot(jnp.concatenate(order[ex : ex + 3], axis=0), wb_ref[ex], preferred_element_type=F32)
        pre_b = part if pre_b is None else pre_b + part
    slope_b = slope(pre_b, sigmoid(pre_b))
    own_g = (up_ref[...].astype(F32) * slope_b[POOL : 2 * POOL]).astype(BF16)
    gbown[...] = own_g
    gy[y] = own_g

    def g_step(k, carry):
        remote(gbown, gy.at[y], BG_Y, {"dp": lax.rem(y + k, ny) * NC + c}).start()
        return carry

    lax.fori_loop(1, ny, g_step, 0)
    u_halo[0].wait_recv()
    u_halo[1].wait_recv()
    left_g = jnp.where(has_left, uph[0].astype(F32) * slope_b[0:POOL], 0.0).astype(BF16)
    right_g = jnp.where(has_right, uph[1].astype(F32) * slope_b[2 * POOL :], 0.0).astype(BF16)

    grad_pool = None
    for ex, plane in ((0, right_g), (1, own_g), (2, left_g)):
        wide = plane.astype(F32)
        moved = [shift_column(wide, -step, HZ) for step in (-1, 0, 1)]
        for ey in range(3):
            for ez in range(3):
                tap = ey * 3 + ez
                shifted = shift_block(moved[ez], -(ey - 1) * HZ).astype(BF16)
                part = lax.dot_general(
                    shifted, wb_ref[ex, tap * 128 : (tap + 1) * 128, :],
                    (((1,), (1,)), ((), ())), preferred_element_type=F32,
                )
                grad_pool = part if grad_pool is None else grad_pool + part

    tall = jnp.broadcast_to(grad_pool.reshape(HY, 1, HZ, 128), (HY, 2, HZ, 128)).reshape(GY * HZ, 128)
    spread[pl.ds(0, GY * HZ, stride=2), :] = tall
    spread[pl.ds(1, GY * HZ, stride=2), :] = tall
    for q in range(2):
        gaown[q] = (spread[...] * slope_a[q * CELLS : (q + 1) * CELLS, :]).astype(BF16)
    a_halo = [start(gaown.at[1], gah.at[0], A_R, {"space": right}), start(gaown.at[0], gah.at[1], A_L, {"space": left})]

    rows_a = 64 // nd
    taps_x = ac_send.shape[3]
    grads = [gaown[0], gaown[1]]
    for tap in range(27, taps_x * NX):
        ac_send[:, :, tap // taps_x, tap % taps_x] = jnp.zeros((NC, ny, rows_a, 128), BF16)
    for ex in range(3):
        for ey in range(3):
            term = None
            for q in range(2):
                part = lax.dot_general(
                    xz[q + ex, ey * GZ : ey * GZ + CELLS, :], grads[q],
                    (((0,), (0,)), ((), ())), preferred_element_type=F32,
                )
                term = part if term is None else term + part
            for ez in range(3):
                tap = ex * 9 + ey * 3 + ez
                ac_send[:, :, tap // taps_x, tap % taps_x] = (
                    term[ez * 64 : (ez + 1) * 64, :].reshape(NC, ny, rows_a, 128).astype(BF16)
                )
    a_core = start(ac_send.at[1 - c], ac_recv, A_C, core)

    def put_gz(q, plane):
        wide = jnp.concatenate([shift_column(plane, 1, GZ), plane, shift_column(plane, -1, GZ)], axis=1)
        gz[q, GZ : GZ + CELLS, :] = wide.astype(BF16)

    put_gz(1, gaown[0].astype(F32))
    put_gz(2, gaown[1].astype(F32))

    a_core.wait_recv()
    ayx_send[...] = (ac_send[c].astype(F32) + ac_recv[...].astype(F32)).astype(BF16)
    me_yx = y * NX + x
    ayx_recv[me_yx] = ayx_send[y, x]

    def yx_step(k, carry):
        k_y, k_x = k // NX, k % NX
        remote(
            ayx_send.at[lax.rem(y + k_y, ny), lax.rem(x + k_x, NX)], ayx_recv.at[me_yx], A_YX, yx_device(k)
        ).start()
        return carry

    lax.fori_loop(1, ny * NX, yx_step, 0)

    wait_part(recv, BP_Y, py.at[:, pl.ds(0, ny - 1)])
    bp_core = start(py.at[1 - c], pc, BP_C, core)
    wait_part(recv, BG_Y, gy.at[pl.ds(0, ny - 1)])
    bg_core = start(gy, gc, BG_C, core)

    def conv_at(q, exs, total):
        for ex in exs:
            for ey in range(3):
                part = lax.dot_general(
                    kr[ex * 3 + ey], gz[q + 2 - ex, (2 - ey) * GZ : (2 - ey) * GZ + CELLS, :],
                    (((1,), (1,)), ((), ())), preferred_element_type=F32,
                )
                total = part if total is None else total + part
        return total

    a_halo[0].wait_recv()
    put_gz(0, jnp.where(has_left, gah[0].astype(F32), 0.0))
    a_halo[1].wait_recv()
    put_gz(3, jnp.where(has_right, gah[1].astype(F32), 0.0))

    bp_core.wait_recv()
    bg_core.wait_recv()
    half = ny * POOL
    lane = lax.broadcasted_iota(jnp.int32, (chans, NC * half), 1)
    row = lane // HZ % HY
    column = lane % HZ
    for ex in range(3):
        flat = jnp.concatenate(
            [py[c, n, ex].astype(F32) for n in range(ny)] + [pc[n, ex].astype(F32) for n in range(ny)], axis=1
        )
        for ey in range(3):
            for ez in range(3):
                step = (ey - 1) * HZ + ez - 1
                inside = (row + ey - 1 >= 0) & (row + ey - 1 < HY) & (column + ez - 1 >= 0) & (column + ez - 1 < HZ)
                moved = flat if step == 0 else pltpu.roll(flat, (-step) % (NC * half), 1)
                tap = ex * 9 + ey * 3 + ez
                pcol[tap * chans : (tap + 1) * chans, :] = jnp.where(inside, moved, 0.0).astype(BF16)
    used = 27 * chans
    padded = pcol.shape[0]
    if padded > used:
        pcol[used:padded, :] = jnp.zeros((padded - used, NC * half), BF16)
    part_b = jnp.dot(pcol[:, 0:half], gy[...].reshape(half, 256), preferred_element_type=F32)
    part_b = part_b + jnp.dot(pcol[:, half:], gc[...].reshape(half, 256), preferred_element_type=F32)
    part_b = part_b.T.reshape(nz, NX, 256 // ns, padded).astype(BF16)
    for xx in range(NX):
        bx_send[xx] = part_b[:, xx]
    bx_recv[x] = bx_send[x]

    def bx_step(k, carry):
        other = lax.rem(x + k, NX)
        remote(bx_send.at[other], bx_recv.at[x], B_X, {"space": z * NX + other}).start()
        return carry

    lax.fori_loop(1, NX, bx_step, 0)

    for q in range(2):
        gi_ref[:, q, :] = conv_at(q, (0, 1, 2), None).astype(BF16)

    wait_part(recv, A_YX, ayx_recv.at[pl.ds(0, ny * NX - 1)])
    total = ayx_recv[0].astype(F32)
    for n in range(1, ny * NX):
        total = total + ayx_recv[n].astype(F32)
    az[z] = total.astype(BF16)

    def z_step(k, carry):
        remote(az.at[z], az.at[z], A_Z, z_device(k)).start()
        return carry

    lax.fori_loop(1, nz, z_step, 0)

    wait_part(recv, B_X, bx_recv.at[pl.ds(0, NX - 1)])
    total_b = bx_recv[0].astype(F32)
    for n in range(1, NX):
        total_b = total_b + bx_recv[n].astype(F32)
    bz_send[...] = total_b.astype(BF16)
    bz_recv[z] = bz_send[z]

    def bz_step(k, carry):
        other = lax.rem(z + k, nz)
        remote(bz_send.at[other], bz_recv.at[z], B_Z, {"space": other * NX + x}).start()
        return carry

    lax.fori_loop(1, nz, bz_step, 0)

    wait_part(recv, A_Z, az.at[pl.ds(0, nz - 1)])
    total = az[0].astype(F32)
    for n in range(1, nz):
        total = total + az[n].astype(F32)
    aout[c, me_yx] = (total * scale_a).astype(BF16)

    def out_step(k, carry):
        remote(aout.at[c, me_yx], aout.at[c, me_yx], A_OUT, yx_device(k)).start()
        return carry

    lax.fori_loop(1, ny * NX, out_step, 0)

    wait_part(recv, B_Z, bz_recv.at[pl.ds(0, nz - 1)])
    total_b = bz_recv[0].astype(F32)
    for n in range(1, nz):
        total_b = total_b + bz_recv[n].astype(F32)
    slice_b = c * ny + y
    bag[slice_b] = (total_b * scale_b).astype(BF16)

    def bag_step(k, carry):
        remote(bag.at[slice_b], bag.at[slice_b], B_OUT, {"dp": lax.rem(d + k, nd)}).start()
        return carry

    lax.fori_loop(1, nd, bag_step, 0)

    wait_part(recv, A_OUT, aout.at[0, pl.ds(0, ny * NX - 1)])
    a_out_core = start(aout.at[c], aout.at[c], A_OUT_C, core)

    wait_part(recv, B_OUT, bag.at[pl.ds(0, nd - 1)])
    for tap in range(27):
        gb_ref[tap] = jnp.concatenate(
            [bag[e, :, tap * chans : (tap + 1) * chans].astype(F32) for e in range(nd)], axis=1
        )
    a_out_core.wait_recv()
    ga_ref[...] = aout[...]

    for copy in started:
        copy.wait_send()
    wait_part(send, BP_Y, py.at[:, pl.ds(0, ny - 1)])
    wait_part(send, BG_Y, gy.at[pl.ds(0, ny - 1)])
    wait_part(send, A_YX, ayx_recv.at[pl.ds(0, ny * NX - 1)])
    wait_part(send, A_Z, az.at[pl.ds(0, nz - 1)])
    wait_part(send, A_OUT, ayx_recv.at[pl.ds(0, ny * NX - 1)])
    wait_part(send, B_X, bx_recv.at[pl.ds(0, NX - 1)])
    wait_part(send, B_Z, bz_recv.at[pl.ds(0, nz - 1)])
    wait_part(send, B_OUT, bag.at[pl.ds(0, nd - 1)])


def body(nd, ns, scale_a, scale_b, features, kernel_a, kernel_b, upstream):
    wa = kernel_a.reshape(9, 192, 128)
    wb = kernel_b.reshape(3, 9 * 128, 256)
    up = upstream[0, :, 0, :].T
    ny, nz = nd // NC, ns // NX
    rows_a = 64 // nd
    chans = 128 // nd
    filters = 256 // ns
    taps_x = -(-27 // NX)
    padded = -(-27 * chans // 128) * 128
    vmem = pl.BlockSpec(memory_space=pltpu.VMEM)
    hbm = pl.BlockSpec(memory_space=pl.ANY)
    block_a = (taps_x, rows_a, 128)
    gi, ga, gb = pl.pallas_call(
        functools.partial(kernel, nd, ns, scale_a, scale_b),
        out_shape=(
            jax.ShapeDtypeStruct((64, 2, CELLS), BF16),
            jax.ShapeDtypeStruct((NC, ny * NX) + block_a, BF16),
            jax.ShapeDtypeStruct((27, filters, 128), F32),
        ),
        in_specs=[hbm] * 4,
        out_specs=(vmem, vmem, vmem),
        scratch_shapes=[
            pltpu.VMEM((64, 2, CELLS), BF16),
            pltpu.VMEM((9, 192, 128), BF16),
            pltpu.VMEM((3, 9 * 128, 256), BF16),
            pltpu.VMEM((POOL, 256), BF16),
            pltpu.VMEM((2, 64, CELLS), BF16),
            pltpu.VMEM((2, 64, CELLS), BF16),
            pltpu.VMEM((2, POOL, 256), BF16),
            pltpu.VMEM((4, CELLS + 2 * GZ, 192), BF16),
            pltpu.VMEM((2 * CELLS, 128), F32),
            pltpu.VMEM((2 * CELLS, 128), F32),
            pltpu.VMEM((POOL, 128), BF16),
            pltpu.VMEM((4, POOL, 128), BF16),
            pltpu.VMEM((POOL, 256), BF16),
            pltpu.VMEM((2, CELLS, 128), BF16),
            pltpu.VMEM((2, CELLS, 128), BF16),
            pltpu.VMEM((4, CELLS + 2 * GZ, 384), BF16),
            pltpu.VMEM((9, 64, 384), BF16),
            pltpu.VMEM((CELLS, 128), F32),
            pltpu.VMEM((NC, ny, 3, chans, POOL), BF16),
            pltpu.VMEM((NC, ny, 3, chans, POOL), BF16),
            pltpu.VMEM((ny, 3, chans, POOL), BF16),
            pltpu.VMEM((ny, POOL, 256), BF16),
            pltpu.VMEM((ny, POOL, 256), BF16),
            pltpu.VMEM((padded, nd * POOL), BF16),
            pltpu.VMEM((NC, ny, NX) + block_a, BF16),
            pltpu.VMEM((ny, NX) + block_a, BF16),
            pltpu.VMEM((ny, NX) + block_a, BF16),
            pltpu.VMEM((ny * NX,) + block_a, BF16),
            pltpu.VMEM((nz,) + block_a, BF16),
            pltpu.VMEM((NC, ny * NX) + block_a, BF16),
            pltpu.VMEM((NX, nz, filters, padded), BF16),
            pltpu.VMEM((NX, nz, filters, padded), BF16),
            pltpu.VMEM((nz, filters, padded), BF16),
            pltpu.VMEM((nz, filters, padded), BF16),
            pltpu.VMEM((nd, filters, padded), BF16),
            pltpu.SemaphoreType.DMA((4,)),
            pltpu.SemaphoreType.DMA((N_SEM,)),
            pltpu.SemaphoreType.DMA((N_SEM,)),
        ],
        compiler_params=pltpu.CompilerParams(collective_id=0, has_side_effects=True),
    )(features[0], wa, wb, up)
    ga = ga.reshape(NC, ny, NX * taps_x, rows_a, 128)[:, :, :27]
    grad_a = jnp.transpose(ga, (2, 0, 1, 3, 4)).reshape(27, 64, 128).astype(F32)
    return gi[None], grad_a, jnp.transpose(gb, (0, 2, 1))


def solution(mesh):
    nd, ns = mesh.shape["dp"], mesh.shape["space"]
    cells_all = nd * 2 * ns * CELLS
    run = functools.partial(body, nd, ns, 1.0 / math.sqrt(cells_all), 1.0 / math.sqrt(cells_all / 8))
    return jax.shard_map(
        run,
        mesh=mesh,
        in_specs=(P("dp", None, "space", None), P(), P(), P("dp", None, "space", None)),
        out_specs=(P("dp", None, "space", None), P(), P(None, None, "space")),
        check_vma=False,
    )
```

```python
import functools
import math

import jax
import jax.numpy as jnp
from jax import lax
from jax.experimental import pallas as pl
from jax.experimental.pallas import tpu as pltpu
from jax.sharding import PartitionSpec as P

GY = 16
GZ = 16
CELLS = GY * GZ
HY = GY // 2
HZ = GZ // 2
POOL = HY * HZ
MESH = pl.DeviceIdType.MESH
F32 = jnp.float32
BF16 = jnp.bfloat16

NC = 2
NX = 4

(
    X_R, X_L, U_R, U_L, P_R, P_L, P_RR, P_LL, A_R, A_L, BP_Y, BG_Y, BP_C, BG_C,
    A_C, A_YX, A_Z, A_OUT, A_OUT_C, B_X, B_Z, B_OUT, N_SEM,
) = range(23)


def sigmoid(value):
    return 1.0 / (1.0 + jnp.exp(-value))


def slope(value, sigma):
    return sigma * (1.0 + value * (1.0 - sigma))


def shift_column(value, step, span):
    if step == 0:
        return value
    rows = value.shape[0]
    column = lax.broadcasted_iota(jnp.int32, value.shape, 0) % span + step
    moved = pltpu.roll(value, (-step) % rows, 0)
    return jnp.where((column >= 0) & (column < span), moved, 0.0)


def shift_block(value, step):
    if step == 0:
        return value
    zeros = jnp.zeros((abs(step), value.shape[1]), value.dtype)
    if step > 0:
        return jnp.concatenate([value[step:], zeros], axis=0)
    return jnp.concatenate([zeros, value[:step]], axis=0)


def kernel(
    nd, ns, scale_a, scale_b,
    x_hbm, wa_hbm, wb_hbm, up_hbm,
    gi_ref, ga_ref, gb_ref,
    x_raw, wa_ref, wb_ref, up_ref, xown, xh, uph, xz, xt, slope_a, act_a, pown, ph, gbown,
    gaown, gah, gz, kr, spread,
    psend, py, pc, gy, gc, pcol, ac_send, ac_recv, ayx_send, ayx_recv, az, aout,
    bx_send, bx_recv, bz_send, bz_recv, bag, load, send, recv,
):
    ny, nz = nd // NC, ns // NX
    s = lax.axis_index("space")
    d = lax.axis_index("dp")
    y, c = d // NC, d % NC
    z, x = s // NX, s % NX
    right = lax.rem(s + 1, ns)
    left = lax.rem(s + ns - 1, ns)
    right2 = lax.rem(s + 2, ns)
    left2 = lax.rem(s + ns - 2, ns)
    has_left = s > 0
    has_right = s < ns - 1
    has_left2 = s > 1
    has_right2 = s < ns - 2
    core = {"dp": y * NC + 1 - c}

    loads = [
        pltpu.make_async_copy(src, dst, load.at[i])
        for i, (src, dst) in enumerate(
            ((x_hbm, x_raw), (up_hbm, up_ref), (wa_hbm, wa_ref), (wb_hbm, wb_ref))
        )
    ]
    for copy in loads:
        copy.start()

    def yx_device(k):
        k_y, k_x = k // NX, k % NX
        return {"dp": lax.rem(y + k_y, ny) * NC + c, "space": z * NX + lax.rem(x + k_x, NX)}

    def z_device(k):
        return {"space": lax.rem(z + k, nz) * NX + x}

    barrier = pltpu.get_barrier_semaphore()

    def greet(device):
        pl.semaphore_signal(barrier, inc=1, device_id=device, device_id_type=MESH)

    for near in (right, left, right2, left2):
        greet({"space": near})

    def greet_yx(k, carry):
        greet(yx_device(k))
        return carry

    def greet_z(k, carry):
        greet(z_device(k))
        return carry

    def greet_dp(k, carry):
        greet({"dp": lax.rem(d + k, nd)})
        return carry

    lax.fori_loop(1, nz, greet_z, 0)
    lax.fori_loop(1, ny * NX, greet_yx, 0)
    lax.fori_loop(1, nd, greet_dp, 0)

    loads[0].wait()
    both = x_raw[...].astype(F32)
    planes = [both[:, 0, :], both[:, 1, :]]
    for q in range(2):
        xown[q] = planes[q].astype(BF16)
    for q in range(4):
        xz[q, 0:GZ, :] = jnp.zeros((GZ, 192), BF16)
        xz[q, GZ + CELLS : 2 * GZ + CELLS, :] = jnp.zeros((GZ, 192), BF16)
        gz[q, 0:GZ, :] = jnp.zeros((GZ, 384), BF16)
        gz[q, GZ + CELLS : 2 * GZ + CELLS, :] = jnp.zeros((GZ, 384), BF16)

    def put_xz(q, plane):
        rows = plane.T
        wide = jnp.concatenate([shift_column(rows, -1, GZ), rows, shift_column(rows, 1, GZ)], axis=1)
        xz[q, GZ : GZ + CELLS, :] = wide.astype(BF16)

    put_xz(1, planes[0])
    put_xz(2, planes[1])
    loads[1].wait()
    loads[2].wait()
    for t in range(9):
        for j in range(3):
            kr[t, :, j * 128 : (j + 1) * 128] = wa_ref[t, j * 64 : (j + 1) * 64, :]

    def conv_a_terms(q, exs):
        total = None
        for ex in exs:
            for ey in range(3):
                part = jnp.dot(
                    xz[q + ex, ey * GZ : ey * GZ + CELLS, :], wa_ref[ex * 3 + ey],
                    preferred_element_type=F32,
                )
                total = part if total is None else total + part
        return total

    pl.semaphore_wait(barrier, 4 + (nz - 1) + (ny * NX - 1) + (nd - 1))

    def remote(src, dst, slot, device):
        return pltpu.make_async_remote_copy(
            src_ref=src, dst_ref=dst, send_sem=send.at[slot], recv_sem=recv.at[slot],
            device_id=device, device_id_type=MESH,
        )

    started = []

    def start(src, dst, slot, device):
        copy = remote(src, dst, slot, device)
        copy.start()
        started.append(copy)
        return copy

    def wait_part(sems, slot, part):
        pltpu.make_async_copy(part, part, sems.at[slot]).wait()

    x_halo = [start(xown.at[1], xh.at[0], X_R, {"space": right}), start(xown.at[0], xh.at[1], X_L, {"space": left})]
    u_halo = [start(up_ref, uph.at[0], U_R, {"space": right}), start(up_ref, uph.at[1], U_L, {"space": left})]

    act_a[0:CELLS, :] = conv_a_terms(0, (1, 2))
    act_a[CELLS : 2 * CELLS, :] = conv_a_terms(1, (0, 1))
    x_halo[0].wait_recv()
    put_xz(0, jnp.where(has_left, xh[0].astype(F32), 0.0))
    x_halo[1].wait_recv()
    put_xz(3, jnp.where(has_right, xh[1].astype(F32), 0.0))
    for q in range(2):
        area = slice(q * CELLS, (q + 1) * CELLS)
        pre = act_a[area, :] + conv_a_terms(q, (0,) if q == 0 else (2,))
        sigma = sigmoid(pre)
        act_a[area, :] = pre * sigma
        slope_a[area, :] = slope(pre, sigma) * 0.125

    pairs = act_a[pl.ds(0, CELLS, stride=2), :] + act_a[pl.ds(1, CELLS, stride=2), :]
    pairs = pairs.reshape(2, HY, 2, HZ, 128)
    pooled = (pairs[0, :, 0] + pairs[0, :, 1] + pairs[1, :, 0] + pairs[1, :, 1]).reshape(POOL, 128) * 0.125
    pown[...] = pooled.astype(BF16)
    p_halo = [
        start(pown, ph.at[0], P_RR, {"space": right2}),
        start(pown, ph.at[3], P_LL, {"space": left2}),
        start(pown, ph.at[1], P_R, {"space": right}),
        start(pown, ph.at[2], P_L, {"space": left}),
    ]

    for q in range(4):
        for ey in range(3):
            rows = xz[q, ey * GZ : ey * GZ + CELLS, :].astype(F32)
            xt[q, ey * 192 : (ey + 1) * 192, :] = rows.T.astype(BF16)

    def taps_of(plane):
        moved = [shift_column(plane, step, HZ) for step in (-1, 0, 1)]
        taps = []
        for ey in range(3):
            for ez in range(3):
                taps.append(shift_block(moved[ez], (ey - 1) * HZ).astype(BF16))
        return jnp.concatenate(taps, axis=1)

    own_p = pown[...].astype(F32)
    own_taps = taps_of(own_p)
    loads[3].wait()
    p_halo[2].wait_recv()
    p_halo[3].wait_recv()
    left_p = jnp.where(has_left, ph[1].astype(F32), 0.0)
    right_p = jnp.where(has_right, ph[2].astype(F32), 0.0)

    chans = 128 // nd
    for e, plane in enumerate((left_p, own_p, right_p)):
        psend[:, :, e] = plane.T.reshape(NC, ny, chans, POOL).astype(BF16)
    for cc in range(NC):
        py[cc, y] = psend[cc, y]

    def p_step(k, carry):
        other = lax.rem(y + k, ny)
        for cc in range(NC):
            remote(psend.at[cc, other], py.at[cc, y], BP_Y, {"dp": other * NC + c}).start()
        return carry

    lax.fori_loop(1, ny, p_step, 0)
    left_taps = taps_of(left_p)
    right_taps = taps_of(right_p)
    p_halo[0].wait_recv()
    p_halo[1].wait_recv()
    left2_taps = taps_of(jnp.where(has_left2, ph[0].astype(F32), 0.0))
    right2_taps = taps_of(jnp.where(has_right2, ph[3].astype(F32), 0.0))
    order = (left2_taps, left_taps, own_taps, right_taps, right2_taps)
    pre_b = None
    for ex in range(3):
        part = jnp.dot(jnp.concatenate(order[ex : ex + 3], axis=0), wb_ref[ex], preferred_element_type=F32)
        pre_b = part if pre_b is None else pre_b + part
    slope_b = slope(pre_b, sigmoid(pre_b))
    own_g = (up_ref[...].astype(F32) * slope_b[POOL : 2 * POOL]).astype(BF16)
    gbown[...] = own_g
    gy[y] = own_g

    def g_step(k, carry):
        remote(gbown, gy.at[y], BG_Y, {"dp": lax.rem(y + k, ny) * NC + c}).start()
        return carry

    lax.fori_loop(1, ny, g_step, 0)
    u_halo[0].wait_recv()
    u_halo[1].wait_recv()
    left_g = jnp.where(has_left, uph[0].astype(F32) * slope_b[0:POOL], 0.0).astype(BF16)
    right_g = jnp.where(has_right, uph[1].astype(F32) * slope_b[2 * POOL :], 0.0).astype(BF16)

    products = None
    for ex, plane in ((0, right_g), (1, own_g), (2, left_g)):
        part = lax.dot_general(
            wb_ref[ex], plane, (((1,), (1,)), ((), ())), preferred_element_type=F32,
        )
        products = part if products is None else products + part
    grad_pool = None
    for ez in range(3):
        column = None
        for ey in range(3):
            tap = ey * 3 + ez
            part = shift_block(products[tap * 128 : (tap + 1) * 128, :].T, -(ey - 1) * HZ)
            column = part if column is None else column + part
        column = shift_column(column, -(ez - 1), HZ)
        grad_pool = column if grad_pool is None else grad_pool + column

    tall = jnp.broadcast_to(grad_pool.reshape(HY, 1, HZ, 128), (HY, 2, HZ, 128)).reshape(GY * HZ, 128)
    spread[pl.ds(0, GY * HZ, stride=2), :] = tall
    spread[pl.ds(1, GY * HZ, stride=2), :] = tall
    for q in range(2):
        gaown[q] = (spread[...] * slope_a[q * CELLS : (q + 1) * CELLS, :]).astype(BF16)
    a_halo = [start(gaown.at[1], gah.at[0], A_R, {"space": right}), start(gaown.at[0], gah.at[1], A_L, {"space": left})]

    rows_a = 64 // nd
    taps_x = ac_send.shape[3]
    grads = [gaown[0], gaown[1]]
    for tap in range(27, taps_x * NX):
        ac_send[:, :, tap // taps_x, tap % taps_x] = jnp.zeros((NC, ny, rows_a, 128), BF16)
    for ex in range(3):
        term = None
        for q in range(2):
            part = jnp.dot(xt[q + ex], grads[q], preferred_element_type=F32)
            term = part if term is None else term + part
        for t in range(9):
            tap = ex * 9 + t
            ac_send[:, :, tap // taps_x, tap % taps_x] = (
                term[t * 64 : (t + 1) * 64, :].reshape(NC, ny, rows_a, 128).astype(BF16)
            )
    a_core = start(ac_send.at[1 - c], ac_recv, A_C, core)

    def put_gz(q, plane):
        wide = jnp.concatenate([shift_column(plane, 1, GZ), plane, shift_column(plane, -1, GZ)], axis=1)
        gz[q, GZ : GZ + CELLS, :] = wide.astype(BF16)

    put_gz(1, gaown[0].astype(F32))
    put_gz(2, gaown[1].astype(F32))

    a_core.wait_recv()
    ayx_send[...] = (ac_send[c].astype(F32) + ac_recv[...].astype(F32)).astype(BF16)
    me_yx = y * NX + x
    ayx_recv[me_yx] = ayx_send[y, x]

    def yx_step(k, carry):
        k_y, k_x = k // NX, k % NX
        remote(
            ayx_send.at[lax.rem(y + k_y, ny), lax.rem(x + k_x, NX)], ayx_recv.at[me_yx], A_YX, yx_device(k)
        ).start()
        return carry

    lax.fori_loop(1, ny * NX, yx_step, 0)

    wait_part(recv, BP_Y, py.at[:, pl.ds(0, ny - 1)])
    bp_core = start(py.at[1 - c], pc, BP_C, core)
    wait_part(recv, BG_Y, gy.at[pl.ds(0, ny - 1)])
    bg_core = start(gy, gc, BG_C, core)

    def conv_at(q, exs, total):
        for ex in exs:
            for ey in range(3):
                part = lax.dot_general(
                    kr[ex * 3 + ey], gz[q + 2 - ex, (2 - ey) * GZ : (2 - ey) * GZ + CELLS, :],
                    (((1,), (1,)), ((), ())), preferred_element_type=F32,
                )
                total = part if total is None else total + part
        return total

    a_halo[0].wait_recv()
    put_gz(0, jnp.where(has_left, gah[0].astype(F32), 0.0))
    a_halo[1].wait_recv()
    put_gz(3, jnp.where(has_right, gah[1].astype(F32), 0.0))

    bp_core.wait_recv()
    bg_core.wait_recv()
    half = ny * POOL
    lane = lax.broadcasted_iota(jnp.int32, (chans, NC * half), 1)
    row = lane // HZ % HY
    column = lane % HZ
    for ex in range(3):
        flat = jnp.concatenate(
            [py[c, n, ex].astype(F32) for n in range(ny)] + [pc[n, ex].astype(F32) for n in range(ny)], axis=1
        )
        for ey in range(3):
            for ez in range(3):
                step = (ey - 1) * HZ + ez - 1
                inside = (row + ey - 1 >= 0) & (row + ey - 1 < HY) & (column + ez - 1 >= 0) & (column + ez - 1 < HZ)
                moved = flat if step == 0 else pltpu.roll(flat, (-step) % (NC * half), 1)
                tap = ex * 9 + ey * 3 + ez
                pcol[tap * chans : (tap + 1) * chans, :] = jnp.where(inside, moved, 0.0).astype(BF16)
    used = 27 * chans
    padded = pcol.shape[0]
    if padded > used:
        pcol[used:padded, :] = jnp.zeros((padded - used, NC * half), BF16)
    part_b = jnp.dot(pcol[:, 0:half], gy[...].reshape(half, 256), preferred_element_type=F32)
    part_b = part_b + jnp.dot(pcol[:, half:], gc[...].reshape(half, 256), preferred_element_type=F32)
    part_b = part_b.T.reshape(nz, NX, 256 // ns, padded).astype(BF16)
    for xx in range(NX):
        bx_send[xx] = part_b[:, xx]
    bx_recv[x] = bx_send[x]

    def bx_step(k, carry):
        other = lax.rem(x + k, NX)
        remote(bx_send.at[other], bx_recv.at[x], B_X, {"space": z * NX + other}).start()
        return carry

    lax.fori_loop(1, NX, bx_step, 0)

    for q in range(2):
        gi_ref[:, q, :] = conv_at(q, (0, 1, 2), None).astype(BF16)

    wait_part(recv, A_YX, ayx_recv.at[pl.ds(0, ny * NX - 1)])
    total = ayx_recv[0].astype(F32)
    for n in range(1, ny * NX):
        total = total + ayx_recv[n].astype(F32)
    az[z] = total.astype(BF16)

    def z_step(k, carry):
        remote(az.at[z], az.at[z], A_Z, z_device(k)).start()
        return carry

    lax.fori_loop(1, nz, z_step, 0)

    wait_part(recv, B_X, bx_recv.at[pl.ds(0, NX - 1)])
    total_b = bx_recv[0].astype(F32)
    for n in range(1, NX):
        total_b = total_b + bx_recv[n].astype(F32)
    bz_send[...] = total_b.astype(BF16)
    bz_recv[z] = bz_send[z]

    def bz_step(k, carry):
        other = lax.rem(z + k, nz)
        remote(bz_send.at[other], bz_recv.at[z], B_Z, {"space": other * NX + x}).start()
        return carry

    lax.fori_loop(1, nz, bz_step, 0)

    wait_part(recv, A_Z, az.at[pl.ds(0, nz - 1)])
    total = az[0].astype(F32)
    for n in range(1, nz):
        total = total + az[n].astype(F32)
    aout[c, me_yx] = (total * scale_a).astype(BF16)

    def out_step(k, carry):
        remote(aout.at[c, me_yx], aout.at[c, me_yx], A_OUT, yx_device(k)).start()
        return carry

    lax.fori_loop(1, ny * NX, out_step, 0)

    wait_part(recv, B_Z, bz_recv.at[pl.ds(0, nz - 1)])
    total_b = bz_recv[0].astype(F32)
    for n in range(1, nz):
        total_b = total_b + bz_recv[n].astype(F32)
    slice_b = c * ny + y
    bag[slice_b] = (total_b * scale_b).astype(BF16)

    def bag_step(k, carry):
        remote(bag.at[slice_b], bag.at[slice_b], B_OUT, {"dp": lax.rem(d + k, nd)}).start()
        return carry

    lax.fori_loop(1, nd, bag_step, 0)

    wait_part(recv, A_OUT, aout.at[0, pl.ds(0, ny * NX - 1)])
    a_out_core = start(aout.at[c], aout.at[c], A_OUT_C, core)

    wait_part(recv, B_OUT, bag.at[pl.ds(0, nd - 1)])
    for tap in range(27):
        gb_ref[tap] = jnp.concatenate(
            [bag[e, :, tap * chans : (tap + 1) * chans].astype(F32) for e in range(nd)], axis=1
        )
    a_out_core.wait_recv()
    ga_ref[...] = aout[...]

    for copy in started:
        copy.wait_send()
    wait_part(send, BP_Y, py.at[:, pl.ds(0, ny - 1)])
    wait_part(send, BG_Y, gy.at[pl.ds(0, ny - 1)])
    wait_part(send, A_YX, ayx_recv.at[pl.ds(0, ny * NX - 1)])
    wait_part(send, A_Z, az.at[pl.ds(0, nz - 1)])
    wait_part(send, A_OUT, ayx_recv.at[pl.ds(0, ny * NX - 1)])
    wait_part(send, B_X, bx_recv.at[pl.ds(0, NX - 1)])
    wait_part(send, B_Z, bz_recv.at[pl.ds(0, nz - 1)])
    wait_part(send, B_OUT, bag.at[pl.ds(0, nd - 1)])


def body(nd, ns, scale_a, scale_b, features, kernel_a, kernel_b, upstream):
    wa = kernel_a.reshape(9, 192, 128)
    wb = kernel_b.reshape(3, 9 * 128, 256)
    up = upstream[0, :, 0, :].T
    ny, nz = nd // NC, ns // NX
    rows_a = 64 // nd
    chans = 128 // nd
    filters = 256 // ns
    taps_x = -(-27 // NX)
    padded = -(-27 * chans // 128) * 128
    vmem = pl.BlockSpec(memory_space=pltpu.VMEM)
    hbm = pl.BlockSpec(memory_space=pl.ANY)
    block_a = (taps_x, rows_a, 128)
    gi, ga, gb = pl.pallas_call(
        functools.partial(kernel, nd, ns, scale_a, scale_b),
        out_shape=(
            jax.ShapeDtypeStruct((64, 2, CELLS), BF16),
            jax.ShapeDtypeStruct((NC, ny * NX) + block_a, BF16),
            jax.ShapeDtypeStruct((27, filters, 128), F32),
        ),
        in_specs=[hbm] * 4,
        out_specs=(vmem, vmem, vmem),
        scratch_shapes=[
            pltpu.VMEM((64, 2, CELLS), BF16),
            pltpu.VMEM((9, 192, 128), BF16),
            pltpu.VMEM((3, 9 * 128, 256), BF16),
            pltpu.VMEM((POOL, 256), BF16),
            pltpu.VMEM((2, 64, CELLS), BF16),
            pltpu.VMEM((2, 64, CELLS), BF16),
            pltpu.VMEM((2, POOL, 256), BF16),
            pltpu.VMEM((4, CELLS + 2 * GZ, 192), BF16),
            pltpu.VMEM((4, 576, CELLS), BF16),
            pltpu.VMEM((2 * CELLS, 128), F32),
            pltpu.VMEM((2 * CELLS, 128), F32),
            pltpu.VMEM((POOL, 128), BF16),
            pltpu.VMEM((4, POOL, 128), BF16),
            pltpu.VMEM((POOL, 256), BF16),
            pltpu.VMEM((2, CELLS, 128), BF16),
            pltpu.VMEM((2, CELLS, 128), BF16),
            pltpu.VMEM((4, CELLS + 2 * GZ, 384), BF16),
            pltpu.VMEM((9, 64, 384), BF16),
            pltpu.VMEM((CELLS, 128), F32),
            pltpu.VMEM((NC, ny, 3, chans, POOL), BF16),
            pltpu.VMEM((NC, ny, 3, chans, POOL), BF16),
            pltpu.VMEM((ny, 3, chans, POOL), BF16),
            pltpu.VMEM((ny, POOL, 256), BF16),
            pltpu.VMEM((ny, POOL, 256), BF16),
            pltpu.VMEM((padded, nd * POOL), BF16),
            pltpu.VMEM((NC, ny, NX) + block_a, BF16),
            pltpu.VMEM((ny, NX) + block_a, BF16),
            pltpu.VMEM((ny, NX) + block_a, BF16),
            pltpu.VMEM((ny * NX,) + block_a, BF16),
            pltpu.VMEM((nz,) + block_a, BF16),
            pltpu.VMEM((NC, ny * NX) + block_a, BF16),
            pltpu.VMEM((NX, nz, filters, padded), BF16),
            pltpu.VMEM((NX, nz, filters, padded), BF16),
            pltpu.VMEM((nz, filters, padded), BF16),
            pltpu.VMEM((nz, filters, padded), BF16),
            pltpu.VMEM((nd, filters, padded), BF16),
            pltpu.SemaphoreType.DMA((4,)),
            pltpu.SemaphoreType.DMA((N_SEM,)),
            pltpu.SemaphoreType.DMA((N_SEM,)),
        ],
        compiler_params=pltpu.CompilerParams(collective_id=0, has_side_effects=True),
    )(features[0], wa, wb, up)
    ga = ga.reshape(NC, ny, NX * taps_x, rows_a, 128)[:, :, :27]
    grad_a = jnp.transpose(ga, (2, 0, 1, 3, 4)).reshape(27, 64, 128).astype(F32)
    return gi[None], grad_a, jnp.transpose(gb, (0, 2, 1))


def solution(mesh):
    nd, ns = mesh.shape["dp"], mesh.shape["space"]
    cells_all = nd * 2 * ns * CELLS
    run = functools.partial(body, nd, ns, 1.0 / math.sqrt(cells_all), 1.0 / math.sqrt(cells_all / 8))
    return jax.shard_map(
        run,
        mesh=mesh,
        in_specs=(P("dp", None, "space", None), P(), P(), P("dp", None, "space", None)),
        out_specs=(P("dp", None, "space", None), P(), P(None, None, "space")),
        check_vma=False,
    )
```

```python
import functools
import math

import jax
import jax.numpy as jnp
from jax import lax
from jax.experimental import pallas as pl
from jax.experimental.pallas import tpu as pltpu
from jax.sharding import PartitionSpec as P

GY = 16
GZ = 16
CELLS = GY * GZ
HY = GY // 2
HZ = GZ // 2
POOL = HY * HZ
MESH = pl.DeviceIdType.MESH
F32 = jnp.float32
BF16 = jnp.bfloat16

NC = 2
NX = 4

(
    X_R, X_L, U_R, U_L, P_R, P_L, P_RR, P_LL, A_R, A_L, BP_Y, BG_Y, BP_C, BG_C,
    A_C, A_YX, A_Z, A_OUT, A_OUT_C, B_X, B_Z, B_OUT, N_SEM,
) = range(23)


def sigmoid(value):
    return 1.0 / (1.0 + jnp.exp(-value))


def slope(value, sigma):
    return sigma * (1.0 + value * (1.0 - sigma))


def shift_column(value, step, span):
    if step == 0:
        return value
    rows = value.shape[0]
    column = lax.broadcasted_iota(jnp.int32, value.shape, 0) % span + step
    moved = pltpu.roll(value, (-step) % rows, 0)
    return jnp.where((column >= 0) & (column < span), moved, 0.0)


def shift_block(value, step):
    if step == 0:
        return value
    zeros = jnp.zeros((abs(step), value.shape[1]), value.dtype)
    if step > 0:
        return jnp.concatenate([value[step:], zeros], axis=0)
    return jnp.concatenate([zeros, value[:step]], axis=0)


def kernel(
    nd, ns, scale_a, scale_b,
    x_hbm, wa_hbm, wb_hbm, up_hbm,
    gi_ref, ga_ref, gb_ref,
    x_raw, wa_ref, wb_ref, up_ref, xown, xh, uph, xz, xt, slope_a, act_a, pown, ph, gbown,
    gaown, gah, gz, kr, spread,
    psend, py, pc, gy, gc, pcol, ac_send, ac_recv, ayx_send, ayx_recv, az, aout,
    bx_send, bx_recv, bz_send, bz_recv, bag, load, send, recv,
):
    ny, nz = nd // NC, ns // NX
    s = lax.axis_index("space")
    d = lax.axis_index("dp")
    y, c = d // NC, d % NC
    z, x = s // NX, s % NX
    right = lax.rem(s + 1, ns)
    left = lax.rem(s + ns - 1, ns)
    right2 = lax.rem(s + 2, ns)
    left2 = lax.rem(s + ns - 2, ns)
    has_left = s > 0
    has_right = s < ns - 1
    has_left2 = s > 1
    has_right2 = s < ns - 2
    core = {"dp": y * NC + 1 - c}

    loads = [
        pltpu.make_async_copy(src, dst, load.at[i])
        for i, (src, dst) in enumerate(
            ((x_hbm, x_raw), (up_hbm, up_ref), (wa_hbm, wa_ref), (wb_hbm, wb_ref))
        )
    ]
    for copy in loads:
        copy.start()

    def yx_device(k):
        k_y, k_x = k // NX, k % NX
        return {"dp": lax.rem(y + k_y, ny) * NC + c, "space": z * NX + lax.rem(x + k_x, NX)}

    def z_device(k):
        return {"space": lax.rem(z + k, nz) * NX + x}

    barrier = pltpu.get_barrier_semaphore()

    def greet(device):
        pl.semaphore_signal(barrier, inc=1, device_id=device, device_id_type=MESH)

    for near in (right, left, right2, left2):
        greet({"space": near})

    def greet_yx(k, carry):
        greet(yx_device(k))
        return carry

    def greet_z(k, carry):
        greet(z_device(k))
        return carry

    def greet_dp(k, carry):
        greet({"dp": lax.rem(d + k, nd)})
        return carry

    lax.fori_loop(1, nz, greet_z, 0)
    lax.fori_loop(1, ny * NX, greet_yx, 0)
    lax.fori_loop(1, nd, greet_dp, 0)

    loads[0].wait()
    both = x_raw[...].astype(F32)
    planes = [both[:, 0, :], both[:, 1, :]]
    for q in range(2):
        xown[q] = planes[q].astype(BF16)
    for q in range(4):
        xz[q, 0:GZ, :] = jnp.zeros((GZ, 192), BF16)
        xz[q, GZ + CELLS : 2 * GZ + CELLS, :] = jnp.zeros((GZ, 192), BF16)
        gz[q, 0:GZ, :] = jnp.zeros((GZ, 384), BF16)
        gz[q, GZ + CELLS : 2 * GZ + CELLS, :] = jnp.zeros((GZ, 384), BF16)

    def put_xz(q, plane):
        rows = plane.T
        wide = jnp.concatenate([shift_column(rows, -1, GZ), rows, shift_column(rows, 1, GZ)], axis=1)
        xz[q, GZ : GZ + CELLS, :] = wide.astype(BF16)

    put_xz(1, planes[0])
    put_xz(2, planes[1])
    loads[1].wait()
    loads[2].wait()
    for t in range(9):
        for j in range(3):
            kr[t, :, j * 128 : (j + 1) * 128] = wa_ref[t, j * 64 : (j + 1) * 64, :]

    def conv_a_terms(q, exs):
        total = None
        for ex in exs:
            for ey in range(3):
                part = jnp.dot(
                    xz[q + ex, ey * GZ : ey * GZ + CELLS, :], wa_ref[ex * 3 + ey],
                    preferred_element_type=F32,
                )
                total = part if total is None else total + part
        return total

    pl.semaphore_wait(barrier, 4 + (nz - 1) + (ny * NX - 1) + (nd - 1))

    def remote(src, dst, slot, device):
        return pltpu.make_async_remote_copy(
            src_ref=src, dst_ref=dst, send_sem=send.at[slot], recv_sem=recv.at[slot],
            device_id=device, device_id_type=MESH,
        )

    started = []

    def start(src, dst, slot, device):
        copy = remote(src, dst, slot, device)
        copy.start()
        started.append(copy)
        return copy

    def wait_part(sems, slot, part):
        pltpu.make_async_copy(part, part, sems.at[slot]).wait()

    x_halo = [start(xown.at[1], xh.at[0], X_R, {"space": right}), start(xown.at[0], xh.at[1], X_L, {"space": left})]
    u_halo = [start(up_ref, uph.at[0], U_R, {"space": right}), start(up_ref, uph.at[1], U_L, {"space": left})]

    act_a[0:CELLS, :] = conv_a_terms(0, (1, 2))
    act_a[CELLS : 2 * CELLS, :] = conv_a_terms(1, (0, 1))
    x_halo[0].wait_recv()
    put_xz(0, jnp.where(has_left, xh[0].astype(F32), 0.0))
    x_halo[1].wait_recv()
    put_xz(3, jnp.where(has_right, xh[1].astype(F32), 0.0))
    for q in range(2):
        area = slice(q * CELLS, (q + 1) * CELLS)
        pre = act_a[area, :] + conv_a_terms(q, (0,) if q == 0 else (2,))
        sigma = sigmoid(pre)
        act_a[area, :] = pre * sigma
        slope_a[area, :] = slope(pre, sigma) * 0.125

    pairs = act_a[pl.ds(0, CELLS, stride=2), :] + act_a[pl.ds(1, CELLS, stride=2), :]
    pairs = pairs.reshape(2, HY, 2, HZ, 128)
    pooled = (pairs[0, :, 0] + pairs[0, :, 1] + pairs[1, :, 0] + pairs[1, :, 1]).reshape(POOL, 128) * 0.125
    pown[...] = pooled.astype(BF16)
    p_halo = [
        start(pown, ph.at[0], P_RR, {"space": right2}),
        start(pown, ph.at[3], P_LL, {"space": left2}),
        start(pown, ph.at[1], P_R, {"space": right}),
        start(pown, ph.at[2], P_L, {"space": left}),
    ]

    for q in range(4):
        for ey in range(3):
            rows = xz[q, ey * GZ : ey * GZ + CELLS, :].astype(F32)
            xt[q, ey * 192 : (ey + 1) * 192, :] = rows.T.astype(BF16)

    def taps_of(plane):
        moved = [shift_column(plane, step, HZ) for step in (-1, 0, 1)]
        taps = []
        for ey in range(3):
            for ez in range(3):
                taps.append(shift_block(moved[ez], (ey - 1) * HZ).astype(BF16))
        return jnp.concatenate(taps, axis=1)

    own_p = pown[...].astype(F32)
    own_taps = taps_of(own_p)
    loads[3].wait()
    p_halo[2].wait_recv()
    p_halo[3].wait_recv()
    left_p = jnp.where(has_left, ph[1].astype(F32), 0.0)
    right_p = jnp.where(has_right, ph[2].astype(F32), 0.0)

    chans = 128 // nd
    for e, plane in enumerate((left_p, own_p, right_p)):
        psend[:, :, e] = plane.T.reshape(NC, ny, chans, POOL).astype(BF16)
    for cc in range(NC):
        py[cc, y] = psend[cc, y]

    def p_step(k, carry):
        other = lax.rem(y + k, ny)
        for cc in range(NC):
            remote(psend.at[cc, other], py.at[cc, y], BP_Y, {"dp": other * NC + c}).start()
        return carry

    lax.fori_loop(1, ny, p_step, 0)
    left_taps = taps_of(left_p)
    right_taps = taps_of(right_p)
    p_halo[0].wait_recv()
    p_halo[1].wait_recv()
    left2_taps = taps_of(jnp.where(has_left2, ph[0].astype(F32), 0.0))
    right2_taps = taps_of(jnp.where(has_right2, ph[3].astype(F32), 0.0))
    order = (left2_taps, left_taps, own_taps, right_taps, right2_taps)
    pre_b = None
    for ex in range(3):
        part = jnp.dot(jnp.concatenate(order[ex : ex + 3], axis=0), wb_ref[ex], preferred_element_type=F32)
        pre_b = part if pre_b is None else pre_b + part
    slope_b = slope(pre_b, sigmoid(pre_b))
    own_g = (up_ref[...].astype(F32) * slope_b[POOL : 2 * POOL]).astype(BF16)
    gbown[...] = own_g
    gy[y] = own_g

    def g_step(k, carry):
        remote(gbown, gy.at[y], BG_Y, {"dp": lax.rem(y + k, ny) * NC + c}).start()
        return carry

    lax.fori_loop(1, ny, g_step, 0)
    u_halo[0].wait_recv()
    u_halo[1].wait_recv()
    left_g = jnp.where(has_left, uph[0].astype(F32) * slope_b[0:POOL], 0.0).astype(BF16)
    right_g = jnp.where(has_right, uph[1].astype(F32) * slope_b[2 * POOL :], 0.0).astype(BF16)

    products = None
    for ex, plane in ((0, right_g), (1, own_g), (2, left_g)):
        part = lax.dot_general(
            wb_ref[ex], plane, (((1,), (1,)), ((), ())), preferred_element_type=F32,
        )
        products = part if products is None else products + part
    grad_pool = None
    for ez in range(3):
        column = None
        for ey in range(3):
            tap = ey * 3 + ez
            part = shift_block(products[tap * 128 : (tap + 1) * 128, :].T, -(ey - 1) * HZ)
            column = part if column is None else column + part
        column = shift_column(column, -(ez - 1), HZ)
        grad_pool = column if grad_pool is None else grad_pool + column

    tall = jnp.broadcast_to(grad_pool.reshape(HY, 1, HZ, 128), (HY, 2, HZ, 128)).reshape(GY * HZ, 128)
    spread[pl.ds(0, GY * HZ, stride=2), :] = tall
    spread[pl.ds(1, GY * HZ, stride=2), :] = tall
    for q in range(2):
        gaown[q] = (spread[...] * slope_a[q * CELLS : (q + 1) * CELLS, :]).astype(BF16)
    a_halo = [start(gaown.at[1], gah.at[0], A_R, {"space": right}), start(gaown.at[0], gah.at[1], A_L, {"space": left})]

    rows_a = 64 // nd
    taps_x = ac_send.shape[3]
    grads = [gaown[0], gaown[1]]
    for tap in range(27, taps_x * NX):
        ac_send[:, :, tap // taps_x, tap % taps_x] = jnp.zeros((NC, ny, rows_a, 128), BF16)
    for ex in range(3):
        term = None
        for q in range(2):
            part = jnp.dot(xt[q + ex], grads[q], preferred_element_type=F32)
            term = part if term is None else term + part
        for t in range(9):
            tap = ex * 9 + t
            ac_send[:, :, tap // taps_x, tap % taps_x] = (
                term[t * 64 : (t + 1) * 64, :].reshape(NC, ny, rows_a, 128).astype(BF16)
            )
    a_core = start(ac_send.at[1 - c], ac_recv, A_C, core)

    def put_gz(q, plane):
        wide = jnp.concatenate([shift_column(plane, 1, GZ), plane, shift_column(plane, -1, GZ)], axis=1)
        gz[q, GZ : GZ + CELLS, :] = wide.astype(BF16)

    put_gz(1, gaown[0].astype(F32))
    put_gz(2, gaown[1].astype(F32))

    a_core.wait_recv()
    ayx_send[...] = (ac_send[c].astype(F32) + ac_recv[...].astype(F32)).astype(BF16)
    me_yx = y * NX + x
    ayx_recv[me_yx] = ayx_send[y, x]

    def yx_step(k, carry):
        k_y, k_x = k // NX, k % NX
        remote(
            ayx_send.at[lax.rem(y + k_y, ny), lax.rem(x + k_x, NX)], ayx_recv.at[me_yx], A_YX, yx_device(k)
        ).start()
        return carry

    lax.fori_loop(1, ny * NX, yx_step, 0)

    wait_part(recv, BP_Y, py.at[:, pl.ds(0, ny - 1)])
    bp_core = start(py.at[1 - c], pc, BP_C, core)

    def conv_at(q, exs, total):
        for ex in exs:
            for ey in range(3):
                part = lax.dot_general(
                    kr[ex * 3 + ey], gz[q + 2 - ex, (2 - ey) * GZ : (2 - ey) * GZ + CELLS, :],
                    (((1,), (1,)), ((), ())), preferred_element_type=F32,
                )
                total = part if total is None else total + part
        return total

    bp_core.wait_recv()
    half = ny * POOL
    lane = lax.broadcasted_iota(jnp.int32, (chans, NC * half), 1)
    row = lane // HZ % HY
    column = lane % HZ
    for ex in range(3):
        if ex == 1:
            wait_part(recv, BG_Y, gy.at[pl.ds(0, ny - 1)])
            bg_core = start(gy, gc, BG_C, core)
        flat = jnp.concatenate(
            [py[c, n, ex].astype(F32) for n in range(ny)] + [pc[n, ex].astype(F32) for n in range(ny)], axis=1
        )
        for ey in range(3):
            for ez in range(3):
                step = (ey - 1) * HZ + ez - 1
                inside = (row + ey - 1 >= 0) & (row + ey - 1 < HY) & (column + ez - 1 >= 0) & (column + ez - 1 < HZ)
                moved = flat if step == 0 else pltpu.roll(flat, (-step) % (NC * half), 1)
                tap = ex * 9 + ey * 3 + ez
                pcol[tap * chans : (tap + 1) * chans, :] = jnp.where(inside, moved, 0.0).astype(BF16)
    used = 27 * chans
    padded = pcol.shape[0]
    if padded > used:
        pcol[used:padded, :] = jnp.zeros((padded - used, NC * half), BF16)
    part_b = jnp.dot(pcol[:, 0:half], gy[...].reshape(half, 256), preferred_element_type=F32)
    bg_core.wait_recv()
    part_b = part_b + jnp.dot(pcol[:, half:], gc[...].reshape(half, 256), preferred_element_type=F32)
    part_b = part_b.T.reshape(nz, NX, 256 // ns, padded).astype(BF16)
    for xx in range(NX):
        bx_send[xx] = part_b[:, xx]
    bx_recv[x] = bx_send[x]

    def bx_step(k, carry):
        other = lax.rem(x + k, NX)
        remote(bx_send.at[other], bx_recv.at[x], B_X, {"space": z * NX + other}).start()
        return carry

    lax.fori_loop(1, NX, bx_step, 0)

    a_halo[0].wait_recv()
    put_gz(0, jnp.where(has_left, gah[0].astype(F32), 0.0))
    a_halo[1].wait_recv()
    put_gz(3, jnp.where(has_right, gah[1].astype(F32), 0.0))

    wait_part(recv, A_YX, ayx_recv.at[pl.ds(0, ny * NX - 1)])
    total = ayx_recv[0].astype(F32)
    for n in range(1, ny * NX):
        total = total + ayx_recv[n].astype(F32)
    az[z] = total.astype(BF16)

    def z_step(k, carry):
        remote(az.at[z], az.at[z], A_Z, z_device(k)).start()
        return carry

    lax.fori_loop(1, nz, z_step, 0)

    gi_ref[:, 0, :] = conv_at(0, (0, 1, 2), None).astype(BF16)

    wait_part(recv, B_X, bx_recv.at[pl.ds(0, NX - 1)])
    total_b = bx_recv[0].astype(F32)
    for n in range(1, NX):
        total_b = total_b + bx_recv[n].astype(F32)
    bz_send[...] = total_b.astype(BF16)
    bz_recv[z] = bz_send[z]

    def bz_step(k, carry):
        other = lax.rem(z + k, nz)
        remote(bz_send.at[other], bz_recv.at[z], B_Z, {"space": other * NX + x}).start()
        return carry

    lax.fori_loop(1, nz, bz_step, 0)

    gi_ref[:, 1, :] = conv_at(1, (0, 1, 2), None).astype(BF16)

    wait_part(recv, A_Z, az.at[pl.ds(0, nz - 1)])
    total = az[0].astype(F32)
    for n in range(1, nz):
        total = total + az[n].astype(F32)
    aout[c, me_yx] = (total * scale_a).astype(BF16)

    def out_step(k, carry):
        remote(aout.at[c, me_yx], aout.at[c, me_yx], A_OUT, yx_device(k)).start()
        return carry

    lax.fori_loop(1, ny * NX, out_step, 0)

    wait_part(recv, B_Z, bz_recv.at[pl.ds(0, nz - 1)])
    total_b = bz_recv[0].astype(F32)
    for n in range(1, nz):
        total_b = total_b + bz_recv[n].astype(F32)
    slice_b = c * ny + y
    bag[slice_b] = (total_b * scale_b).astype(BF16)

    def bag_step(k, carry):
        remote(bag.at[slice_b], bag.at[slice_b], B_OUT, {"dp": lax.rem(d + k, nd)}).start()
        return carry

    lax.fori_loop(1, nd, bag_step, 0)

    wait_part(recv, A_OUT, aout.at[0, pl.ds(0, ny * NX - 1)])
    a_out_core = start(aout.at[c], aout.at[c], A_OUT_C, core)

    wait_part(recv, B_OUT, bag.at[pl.ds(0, nd - 1)])
    for tap in range(27):
        gb_ref[tap] = jnp.concatenate(
            [bag[e, :, tap * chans : (tap + 1) * chans].astype(F32) for e in range(nd)], axis=1
        )
    a_out_core.wait_recv()
    ga_ref[...] = aout[...]

    for copy in started:
        copy.wait_send()
    wait_part(send, BP_Y, py.at[:, pl.ds(0, ny - 1)])
    wait_part(send, BG_Y, gy.at[pl.ds(0, ny - 1)])
    wait_part(send, A_YX, ayx_recv.at[pl.ds(0, ny * NX - 1)])
    wait_part(send, A_Z, az.at[pl.ds(0, nz - 1)])
    wait_part(send, A_OUT, ayx_recv.at[pl.ds(0, ny * NX - 1)])
    wait_part(send, B_X, bx_recv.at[pl.ds(0, NX - 1)])
    wait_part(send, B_Z, bz_recv.at[pl.ds(0, nz - 1)])
    wait_part(send, B_OUT, bag.at[pl.ds(0, nd - 1)])


def body(nd, ns, scale_a, scale_b, features, kernel_a, kernel_b, upstream):
    wa = kernel_a.reshape(9, 192, 128)
    wb = kernel_b.reshape(3, 9 * 128, 256)
    up = upstream[0, :, 0, :].T
    ny, nz = nd // NC, ns // NX
    rows_a = 64 // nd
    chans = 128 // nd
    filters = 256 // ns
    taps_x = -(-27 // NX)
    padded = -(-27 * chans // 128) * 128
    vmem = pl.BlockSpec(memory_space=pltpu.VMEM)
    hbm = pl.BlockSpec(memory_space=pl.ANY)
    block_a = (taps_x, rows_a, 128)
    gi, ga, gb = pl.pallas_call(
        functools.partial(kernel, nd, ns, scale_a, scale_b),
        out_shape=(
            jax.ShapeDtypeStruct((64, 2, CELLS), BF16),
            jax.ShapeDtypeStruct((NC, ny * NX) + block_a, BF16),
            jax.ShapeDtypeStruct((27, filters, 128), F32),
        ),
        in_specs=[hbm] * 4,
        out_specs=(vmem, vmem, vmem),
        scratch_shapes=[
            pltpu.VMEM((64, 2, CELLS), BF16),
            pltpu.VMEM((9, 192, 128), BF16),
            pltpu.VMEM((3, 9 * 128, 256), BF16),
            pltpu.VMEM((POOL, 256), BF16),
            pltpu.VMEM((2, 64, CELLS), BF16),
            pltpu.VMEM((2, 64, CELLS), BF16),
            pltpu.VMEM((2, POOL, 256), BF16),
            pltpu.VMEM((4, CELLS + 2 * GZ, 192), BF16),
            pltpu.VMEM((4, 576, CELLS), BF16),
            pltpu.VMEM((2 * CELLS, 128), F32),
            pltpu.VMEM((2 * CELLS, 128), F32),
            pltpu.VMEM((POOL, 128), BF16),
            pltpu.VMEM((4, POOL, 128), BF16),
            pltpu.VMEM((POOL, 256), BF16),
            pltpu.VMEM((2, CELLS, 128), BF16),
            pltpu.VMEM((2, CELLS, 128), BF16),
            pltpu.VMEM((4, CELLS + 2 * GZ, 384), BF16),
            pltpu.VMEM((9, 64, 384), BF16),
            pltpu.VMEM((CELLS, 128), F32),
            pltpu.VMEM((NC, ny, 3, chans, POOL), BF16),
            pltpu.VMEM((NC, ny, 3, chans, POOL), BF16),
            pltpu.VMEM((ny, 3, chans, POOL), BF16),
            pltpu.VMEM((ny, POOL, 256), BF16),
            pltpu.VMEM((ny, POOL, 256), BF16),
            pltpu.VMEM((padded, nd * POOL), BF16),
            pltpu.VMEM((NC, ny, NX) + block_a, BF16),
            pltpu.VMEM((ny, NX) + block_a, BF16),
            pltpu.VMEM((ny, NX) + block_a, BF16),
            pltpu.VMEM((ny * NX,) + block_a, BF16),
            pltpu.VMEM((nz,) + block_a, BF16),
            pltpu.VMEM((NC, ny * NX) + block_a, BF16),
            pltpu.VMEM((NX, nz, filters, padded), BF16),
            pltpu.VMEM((NX, nz, filters, padded), BF16),
            pltpu.VMEM((nz, filters, padded), BF16),
            pltpu.VMEM((nz, filters, padded), BF16),
            pltpu.VMEM((nd, filters, padded), BF16),
            pltpu.SemaphoreType.DMA((4,)),
            pltpu.SemaphoreType.DMA((N_SEM,)),
            pltpu.SemaphoreType.DMA((N_SEM,)),
        ],
        compiler_params=pltpu.CompilerParams(collective_id=0, has_side_effects=True),
    )(features[0], wa, wb, up)
    ga = ga.reshape(NC, ny, NX * taps_x, rows_a, 128)[:, :, :27]
    grad_a = jnp.transpose(ga, (2, 0, 1, 3, 4)).reshape(27, 64, 128).astype(F32)
    return gi[None], grad_a, jnp.transpose(gb, (0, 2, 1))


def solution(mesh):
    nd, ns = mesh.shape["dp"], mesh.shape["space"]
    cells_all = nd * 2 * ns * CELLS
    run = functools.partial(body, nd, ns, 1.0 / math.sqrt(cells_all), 1.0 / math.sqrt(cells_all / 8))
    return jax.shard_map(
        run,
        mesh=mesh,
        in_specs=(P("dp", None, "space", None), P(), P(), P("dp", None, "space", None)),
        out_specs=(P("dp", None, "space", None), P(), P(None, None, "space")),
        check_vma=False,
    )
```

```python
import functools
import math

import jax
import jax.numpy as jnp
from jax import lax
from jax.experimental import pallas as pl
from jax.experimental.pallas import tpu as pltpu
from jax.sharding import PartitionSpec as P

GY = 16
GZ = 16
CELLS = GY * GZ
HY = GY // 2
HZ = GZ // 2
POOL = HY * HZ
MESH = pl.DeviceIdType.MESH
F32 = jnp.float32
BF16 = jnp.bfloat16

NC = 2
NX = 4

(
    X_R, X_L, U_R, U_L, P_R, P_L, P_RR, P_LL, A_R, A_L, BP_Y, BG_Y, BP_C, BG_C,
    A_C, A_YX, A_Z, A_OUT, A_OUT_C, B_X, B_Z, B_OUT, N_SEM,
) = range(23)


def sigmoid(value):
    return 1.0 / (1.0 + jnp.exp(-value))


def slope(value, sigma):
    return sigma * (1.0 + value * (1.0 - sigma))


def shift_column(value, step, span):
    if step == 0:
        return value
    rows = value.shape[0]
    column = lax.broadcasted_iota(jnp.int32, value.shape, 0) % span + step
    moved = pltpu.roll(value, (-step) % rows, 0)
    return jnp.where((column >= 0) & (column < span), moved, 0.0)


def shift_block(value, step):
    if step == 0:
        return value
    zeros = jnp.zeros((abs(step), value.shape[1]), value.dtype)
    if step > 0:
        return jnp.concatenate([value[step:], zeros], axis=0)
    return jnp.concatenate([zeros, value[:step]], axis=0)


def kernel(
    nd, ns, scale_a, scale_b,
    x_hbm, wa_hbm, wb_hbm, up_hbm,
    gi_ref, ga_ref, gb_ref,
    x_raw, wa_ref, wb_ref, up_ref, xown, xh, uph, xz, xt, slope_a, act_a, pown, ph, gbown,
    gaown, gah, gz, kr, spread,
    psend, py, pc, gy, gc, pcol, ac_send, ac_recv, ayx_send, ayx_recv, az, aout,
    bx_send, bx_recv, bz_send, bz_recv, bag, load, send, recv,
):
    ny, nz = nd // NC, ns // NX
    s = lax.axis_index("space")
    d = lax.axis_index("dp")
    y, c = d // NC, d % NC
    z, x = s // NX, s % NX
    right = lax.rem(s + 1, ns)
    left = lax.rem(s + ns - 1, ns)
    right2 = lax.rem(s + 2, ns)
    left2 = lax.rem(s + ns - 2, ns)
    has_left = s > 0
    has_right = s < ns - 1
    has_left2 = s > 1
    has_right2 = s < ns - 2
    core = {"dp": y * NC + 1 - c}

    loads = [
        pltpu.make_async_copy(src, dst, load.at[i])
        for i, (src, dst) in enumerate(
            ((x_hbm, x_raw), (up_hbm, up_ref), (wa_hbm, wa_ref), (wb_hbm, wb_ref))
        )
    ]
    for copy in loads:
        copy.start()

    def yx_device(k):
        k_y, k_x = k // NX, k % NX
        return {"dp": lax.rem(y + k_y, ny) * NC + c, "space": z * NX + lax.rem(x + k_x, NX)}

    def z_device(k):
        return {"space": lax.rem(z + k, nz) * NX + x}

    barrier = pltpu.get_barrier_semaphore()

    def greet(device):
        pl.semaphore_signal(barrier, inc=1, device_id=device, device_id_type=MESH)

    for near in (right, left, right2, left2):
        greet({"space": near})

    def greet_yx(k, carry):
        greet(yx_device(k))
        return carry

    def greet_z(k, carry):
        greet(z_device(k))
        return carry

    def greet_dp(k, carry):
        greet({"dp": lax.rem(d + k, nd)})
        return carry

    lax.fori_loop(1, nz, greet_z, 0)
    lax.fori_loop(1, ny * NX, greet_yx, 0)
    lax.fori_loop(1, nd, greet_dp, 0)

    loads[0].wait()
    both = x_raw[...].astype(F32)
    planes = [both[:, 0, :], both[:, 1, :]]
    for q in range(2):
        xown[q] = planes[q].astype(BF16)
    for q in range(4):
        xz[q, 0:GZ, :] = jnp.zeros((GZ, 192), BF16)
        xz[q, GZ + CELLS : 2 * GZ + CELLS, :] = jnp.zeros((GZ, 192), BF16)
        gz[q, 0:GZ, :] = jnp.zeros((GZ, 384), BF16)
        gz[q, GZ + CELLS : 2 * GZ + CELLS, :] = jnp.zeros((GZ, 384), BF16)

    def put_xz(q, plane):
        rows = plane.T
        wide = jnp.concatenate([shift_column(rows, -1, GZ), rows, shift_column(rows, 1, GZ)], axis=1)
        xz[q, GZ : GZ + CELLS, :] = wide.astype(BF16)

    put_xz(1, planes[0])
    put_xz(2, planes[1])
    loads[1].wait()
    loads[2].wait()
    for t in range(9):
        for j in range(3):
            kr[t, :, j * 128 : (j + 1) * 128] = wa_ref[t, j * 64 : (j + 1) * 64, :]

    def conv_a_terms(q, exs):
        total = None
        for ex in exs:
            for ey in range(3):
                part = jnp.dot(
                    xz[q + ex, ey * GZ : ey * GZ + CELLS, :], wa_ref[ex * 3 + ey],
                    preferred_element_type=F32,
                )
                total = part if total is None else total + part
        return total

    pl.semaphore_wait(barrier, 4 + (nz - 1) + (ny * NX - 1) + (nd - 1))

    def remote(src, dst, slot, device):
        return pltpu.make_async_remote_copy(
            src_ref=src, dst_ref=dst, send_sem=send.at[slot], recv_sem=recv.at[slot],
            device_id=device, device_id_type=MESH,
        )

    started = []

    def start(src, dst, slot, device):
        copy = remote(src, dst, slot, device)
        copy.start()
        started.append(copy)
        return copy

    def wait_part(sems, slot, part):
        pltpu.make_async_copy(part, part, sems.at[slot]).wait()

    x_halo = [start(xown.at[1], xh.at[0], X_R, {"space": right}), start(xown.at[0], xh.at[1], X_L, {"space": left})]
    u_halo = [start(up_ref, uph.at[0], U_R, {"space": right}), start(up_ref, uph.at[1], U_L, {"space": left})]

    act_a[0:CELLS, :] = conv_a_terms(0, (1, 2))
    act_a[CELLS : 2 * CELLS, :] = conv_a_terms(1, (0, 1))
    x_halo[0].wait_recv()
    put_xz(0, jnp.where(has_left, xh[0].astype(F32), 0.0))
    x_halo[1].wait_recv()
    put_xz(3, jnp.where(has_right, xh[1].astype(F32), 0.0))
    for q in range(2):
        area = slice(q * CELLS, (q + 1) * CELLS)
        pre = act_a[area, :] + conv_a_terms(q, (0,) if q == 0 else (2,))
        sigma = sigmoid(pre)
        act_a[area, :] = pre * sigma
        slope_a[area, :] = slope(pre, sigma) * 0.125

    pairs = act_a[pl.ds(0, CELLS, stride=2), :] + act_a[pl.ds(1, CELLS, stride=2), :]
    pairs = pairs.reshape(2, HY, 2, HZ, 128)
    pooled = (pairs[0, :, 0] + pairs[0, :, 1] + pairs[1, :, 0] + pairs[1, :, 1]).reshape(POOL, 128) * 0.125
    pown[...] = pooled.astype(BF16)
    p_halo = [
        start(pown, ph.at[0], P_RR, {"space": right2}),
        start(pown, ph.at[3], P_LL, {"space": left2}),
        start(pown, ph.at[1], P_R, {"space": right}),
        start(pown, ph.at[2], P_L, {"space": left}),
    ]

    for q in range(4):
        for ey in range(3):
            rows = xz[q, ey * GZ : ey * GZ + CELLS, :].astype(F32)
            xt[q, ey * 192 : (ey + 1) * 192, :] = rows.T.astype(BF16)

    def taps_of(plane):
        moved = [shift_column(plane, step, HZ) for step in (-1, 0, 1)]
        taps = []
        for ey in range(3):
            for ez in range(3):
                taps.append(shift_block(moved[ez], (ey - 1) * HZ).astype(BF16))
        return jnp.concatenate(taps, axis=1)

    own_p = pown[...].astype(F32)
    own_taps = taps_of(own_p)
    loads[3].wait()
    p_halo[2].wait_recv()
    p_halo[3].wait_recv()
    left_p = jnp.where(has_left, ph[1].astype(F32), 0.0)
    right_p = jnp.where(has_right, ph[2].astype(F32), 0.0)

    chans = 128 // nd
    for e, plane in enumerate((left_p, own_p, right_p)):
        psend[:, :, e] = plane.T.reshape(NC, ny, chans, POOL).astype(BF16)
    for cc in range(NC):
        py[cc, y] = psend[cc, y]

    def p_step(k, carry):
        other = lax.rem(y + k, ny)
        for cc in range(NC):
            remote(psend.at[cc, other], py.at[cc, y], BP_Y, {"dp": other * NC + c}).start()
        return carry

    lax.fori_loop(1, ny, p_step, 0)
    left_taps = taps_of(left_p)
    right_taps = taps_of(right_p)
    p_halo[0].wait_recv()
    p_halo[1].wait_recv()
    left2_taps = taps_of(jnp.where(has_left2, ph[0].astype(F32), 0.0))
    right2_taps = taps_of(jnp.where(has_right2, ph[3].astype(F32), 0.0))
    order = (left2_taps, left_taps, own_taps, right_taps, right2_taps)
    pre_b = None
    for ex in range(3):
        part = jnp.dot(jnp.concatenate(order[ex : ex + 3], axis=0), wb_ref[ex], preferred_element_type=F32)
        pre_b = part if pre_b is None else pre_b + part
    slope_b = slope(pre_b, sigmoid(pre_b))
    own_g = (up_ref[...].astype(F32) * slope_b[POOL : 2 * POOL]).astype(BF16)
    gbown[...] = own_g
    gy[y] = own_g

    def g_step(k, carry):
        remote(gbown, gy.at[y], BG_Y, {"dp": lax.rem(y + k, ny) * NC + c}).start()
        return carry

    lax.fori_loop(1, ny, g_step, 0)
    u_halo[0].wait_recv()
    u_halo[1].wait_recv()
    left_g = jnp.where(has_left, uph[0].astype(F32) * slope_b[0:POOL], 0.0).astype(BF16)
    right_g = jnp.where(has_right, uph[1].astype(F32) * slope_b[2 * POOL :], 0.0).astype(BF16)

    products = None
    for ex, plane in ((0, right_g), (1, own_g), (2, left_g)):
        part = lax.dot_general(
            wb_ref[ex], plane, (((1,), (1,)), ((), ())), preferred_element_type=F32,
        )
        products = part if products is None else products + part
    grad_pool = None
    for ez in range(3):
        column = None
        for ey in range(3):
            tap = ey * 3 + ez
            part = shift_block(products[tap * 128 : (tap + 1) * 128, :].T, -(ey - 1) * HZ)
            column = part if column is None else column + part
        column = shift_column(column, -(ez - 1), HZ)
        grad_pool = column if grad_pool is None else grad_pool + column

    tall = jnp.broadcast_to(grad_pool.reshape(HY, 1, HZ, 128), (HY, 2, HZ, 128)).reshape(GY * HZ, 128)
    spread[pl.ds(0, GY * HZ, stride=2), :] = tall
    spread[pl.ds(1, GY * HZ, stride=2), :] = tall
    for q in range(2):
        gaown[q] = (spread[...] * slope_a[q * CELLS : (q + 1) * CELLS, :]).astype(BF16)
    a_halo = [start(gaown.at[1], gah.at[0], A_R, {"space": right}), start(gaown.at[0], gah.at[1], A_L, {"space": left})]

    rows_a = 64 // nd
    taps_x = ac_send.shape[3]
    grads = [gaown[0], gaown[1]]
    for tap in range(27, taps_x * NX):
        ac_send[:, :, tap // taps_x, tap % taps_x] = jnp.zeros((NC, ny, rows_a, 128), BF16)
    for ex in range(3):
        term = None
        for q in range(2):
            part = jnp.dot(xt[q + ex], grads[q], preferred_element_type=F32)
            term = part if term is None else term + part
        for t in range(9):
            tap = ex * 9 + t
            ac_send[:, :, tap // taps_x, tap % taps_x] = (
                term[t * 64 : (t + 1) * 64, :].reshape(NC, ny, rows_a, 128).astype(BF16)
            )
    a_core = start(ac_send.at[1 - c], ac_recv, A_C, core)

    def put_gz(q, plane):
        wide = jnp.concatenate([shift_column(plane, 1, GZ), plane, shift_column(plane, -1, GZ)], axis=1)
        gz[q, GZ : GZ + CELLS, :] = wide.astype(BF16)

    put_gz(1, gaown[0].astype(F32))
    put_gz(2, gaown[1].astype(F32))

    a_core.wait_recv()
    ayx_send[...] = (ac_send[c].astype(F32) + ac_recv[...].astype(F32)).astype(BF16)
    me_yx = y * NX + x
    ayx_recv[me_yx] = ayx_send[y, x]

    def yx_step(k, carry):
        k_y, k_x = k // NX, k % NX
        remote(
            ayx_send.at[lax.rem(y + k_y, ny), lax.rem(x + k_x, NX)], ayx_recv.at[me_yx], A_YX, yx_device(k)
        ).start()
        return carry

    lax.fori_loop(1, ny * NX, yx_step, 0)

    wait_part(recv, BP_Y, py.at[:, pl.ds(0, ny - 1)])
    bp_core = start(py.at[1 - c], pc, BP_C, core)

    def conv_at(q, exs, total):
        for ex in exs:
            for ey in range(3):
                part = lax.dot_general(
                    kr[ex * 3 + ey], gz[q + 2 - ex, (2 - ey) * GZ : (2 - ey) * GZ + CELLS, :],
                    (((1,), (1,)), ((), ())), preferred_element_type=F32,
                )
                total = part if total is None else total + part
        return total

    bp_core.wait_recv()
    half = ny * POOL
    lane = lax.broadcasted_iota(jnp.int32, (chans, NC * half), 1)
    row = lane // HZ % HY
    column = lane % HZ
    for ex in range(3):
        if ex == 1:
            wait_part(recv, BG_Y, gy.at[pl.ds(0, ny - 1)])
            bg_core = start(gy, gc, BG_C, core)
        flat = jnp.concatenate(
            [py[c, n, ex].astype(F32) for n in range(ny)] + [pc[n, ex].astype(F32) for n in range(ny)], axis=1
        )
        for ey in range(3):
            for ez in range(3):
                step = (ey - 1) * HZ + ez - 1
                inside = (row + ey - 1 >= 0) & (row + ey - 1 < HY) & (column + ez - 1 >= 0) & (column + ez - 1 < HZ)
                moved = flat if step == 0 else pltpu.roll(flat, (-step) % (NC * half), 1)
                tap = ex * 9 + ey * 3 + ez
                pcol[tap * chans : (tap + 1) * chans, :] = jnp.where(inside, moved, 0.0).astype(BF16)
    used = 27 * chans
    padded = pcol.shape[0]
    if padded > used:
        pcol[used:padded, :] = jnp.zeros((padded - used, NC * half), BF16)
    part_b = jnp.dot(pcol[:, 0:half], gy[...].reshape(half, 256), preferred_element_type=F32)
    bg_core.wait_recv()
    part_b = part_b + jnp.dot(pcol[:, half:], gc[...].reshape(half, 256), preferred_element_type=F32)
    part_b = part_b.T.reshape(nz, NX, 256 // ns, padded).astype(BF16)
    for xx in range(NX):
        bx_send[xx] = part_b[:, xx]
    bx_recv[x] = bx_send[x]

    def bx_step(k, carry):
        other = lax.rem(x + k, NX)
        remote(bx_send.at[other], bx_recv.at[x], B_X, {"space": z * NX + other}).start()
        return carry

    lax.fori_loop(1, NX, bx_step, 0)

    a_halo[0].wait_recv()
    put_gz(0, jnp.where(has_left, gah[0].astype(F32), 0.0))
    a_halo[1].wait_recv()
    put_gz(3, jnp.where(has_right, gah[1].astype(F32), 0.0))

    wait_part(recv, A_YX, ayx_recv.at[pl.ds(0, ny * NX - 1)])
    total = ayx_recv[0].astype(F32)
    for n in range(1, ny * NX):
        total = total + ayx_recv[n].astype(F32)
    az[z] = total.astype(BF16)

    def z_step(k, carry):
        remote(az.at[z], az.at[z], A_Z, z_device(k)).start()
        return carry

    lax.fori_loop(1, nz, z_step, 0)

    gi_ref[:, 0, :] = conv_at(0, (0, 1, 2), None).astype(BF16)

    wait_part(recv, B_X, bx_recv.at[pl.ds(0, NX - 1)])
    total_b = bx_recv[0].astype(F32)
    for n in range(1, NX):
        total_b = total_b + bx_recv[n].astype(F32)
    bz_send[...] = total_b.astype(BF16)
    bz_recv[z] = bz_send[z]

    def bz_step(k, carry):
        other = lax.rem(z + k, nz)
        remote(bz_send.at[other], bz_recv.at[z], B_Z, {"space": other * NX + x}).start()
        return carry

    lax.fori_loop(1, nz, bz_step, 0)

    gi_ref[:, 1, :] = conv_at(1, (0, 1, 2), None).astype(BF16)

    wait_part(recv, A_Z, az.at[pl.ds(0, nz - 1)])
    total = az[0].astype(F32)
    for n in range(1, nz):
        total = total + az[n].astype(F32)
    aout[c, me_yx] = (total * scale_a).astype(BF16)

    def out_step(k, carry):
        remote(aout.at[c, me_yx], aout.at[c, me_yx], A_OUT, yx_device(k)).start()
        return carry

    lax.fori_loop(1, ny * NX, out_step, 0)

    wait_part(recv, B_Z, bz_recv.at[pl.ds(0, nz - 1)])
    total_b = bz_recv[0].astype(F32)
    for n in range(1, nz):
        total_b = total_b + bz_recv[n].astype(F32)
    slice_b = c * ny + y
    bag[slice_b] = (total_b * scale_b).astype(BF16)

    def bag_step(k, carry):
        remote(bag.at[slice_b], bag.at[slice_b], B_OUT, {"dp": lax.rem(d + k, nd)}).start()
        return carry

    lax.fori_loop(1, nd, bag_step, 0)

    wait_part(recv, A_OUT, aout.at[0, pl.ds(0, ny * NX - 1)])
    a_out_core = start(aout.at[c], aout.at[c], A_OUT_C, core)

    def put_ga(core_part):
        for n in range(ny):
            rows = pl.ds(pl.multiple_of((core_part * ny + n) * rows_a, rows_a), rows_a)
            for xx in range(NX):
                some = min(taps_x, 27 - xx * taps_x)
                part = aout[core_part, n * NX + xx, 0:some]
                ga_ref[xx * taps_x : xx * taps_x + some, rows, :] = part.astype(F32)

    put_ga(c)

    wait_part(recv, B_OUT, bag.at[pl.ds(0, nd - 1)])
    for tap in range(27):
        gb_ref[tap] = jnp.concatenate(
            [bag[e, :, tap * chans : (tap + 1) * chans].astype(F32) for e in range(nd)], axis=1
        )
    a_out_core.wait_recv()
    put_ga(1 - c)

    for copy in started:
        copy.wait_send()
    wait_part(send, BP_Y, py.at[:, pl.ds(0, ny - 1)])
    wait_part(send, BG_Y, gy.at[pl.ds(0, ny - 1)])
    wait_part(send, A_YX, ayx_recv.at[pl.ds(0, ny * NX - 1)])
    wait_part(send, A_Z, az.at[pl.ds(0, nz - 1)])
    wait_part(send, A_OUT, ayx_recv.at[pl.ds(0, ny * NX - 1)])
    wait_part(send, B_X, bx_recv.at[pl.ds(0, NX - 1)])
    wait_part(send, B_Z, bz_recv.at[pl.ds(0, nz - 1)])
    wait_part(send, B_OUT, bag.at[pl.ds(0, nd - 1)])


def body(nd, ns, scale_a, scale_b, features, kernel_a, kernel_b, upstream):
    wa = kernel_a.reshape(9, 192, 128)
    wb = kernel_b.reshape(3, 9 * 128, 256)
    up = upstream[0, :, 0, :].T
    ny, nz = nd // NC, ns // NX
    rows_a = 64 // nd
    chans = 128 // nd
    filters = 256 // ns
    taps_x = -(-27 // NX)
    padded = -(-27 * chans // 128) * 128
    vmem = pl.BlockSpec(memory_space=pltpu.VMEM)
    hbm = pl.BlockSpec(memory_space=pl.ANY)
    block_a = (taps_x, rows_a, 128)
    gi, ga, gb = pl.pallas_call(
        functools.partial(kernel, nd, ns, scale_a, scale_b),
        out_shape=(
            jax.ShapeDtypeStruct((64, 2, CELLS), BF16),
            jax.ShapeDtypeStruct((27, 64, 128), F32),
            jax.ShapeDtypeStruct((27, filters, 128), F32),
        ),
        in_specs=[hbm] * 4,
        out_specs=(vmem, vmem, vmem),
        scratch_shapes=[
            pltpu.VMEM((64, 2, CELLS), BF16),
            pltpu.VMEM((9, 192, 128), BF16),
            pltpu.VMEM((3, 9 * 128, 256), BF16),
            pltpu.VMEM((POOL, 256), BF16),
            pltpu.VMEM((2, 64, CELLS), BF16),
            pltpu.VMEM((2, 64, CELLS), BF16),
            pltpu.VMEM((2, POOL, 256), BF16),
            pltpu.VMEM((4, CELLS + 2 * GZ, 192), BF16),
            pltpu.VMEM((4, 576, CELLS), BF16),
            pltpu.VMEM((2 * CELLS, 128), F32),
            pltpu.VMEM((2 * CELLS, 128), F32),
            pltpu.VMEM((POOL, 128), BF16),
            pltpu.VMEM((4, POOL, 128), BF16),
            pltpu.VMEM((POOL, 256), BF16),
            pltpu.VMEM((2, CELLS, 128), BF16),
            pltpu.VMEM((2, CELLS, 128), BF16),
            pltpu.VMEM((4, CELLS + 2 * GZ, 384), BF16),
            pltpu.VMEM((9, 64, 384), BF16),
            pltpu.VMEM((CELLS, 128), F32),
            pltpu.VMEM((NC, ny, 3, chans, POOL), BF16),
            pltpu.VMEM((NC, ny, 3, chans, POOL), BF16),
            pltpu.VMEM((ny, 3, chans, POOL), BF16),
            pltpu.VMEM((ny, POOL, 256), BF16),
            pltpu.VMEM((ny, POOL, 256), BF16),
            pltpu.VMEM((padded, nd * POOL), BF16),
            pltpu.VMEM((NC, ny, NX) + block_a, BF16),
            pltpu.VMEM((ny, NX) + block_a, BF16),
            pltpu.VMEM((ny, NX) + block_a, BF16),
            pltpu.VMEM((ny * NX,) + block_a, BF16),
            pltpu.VMEM((nz,) + block_a, BF16),
            pltpu.VMEM((NC, ny * NX) + block_a, BF16),
            pltpu.VMEM((NX, nz, filters, padded), BF16),
            pltpu.VMEM((NX, nz, filters, padded), BF16),
            pltpu.VMEM((nz, filters, padded), BF16),
            pltpu.VMEM((nz, filters, padded), BF16),
            pltpu.VMEM((nd, filters, padded), BF16),
            pltpu.SemaphoreType.DMA((4,)),
            pltpu.SemaphoreType.DMA((N_SEM,)),
            pltpu.SemaphoreType.DMA((N_SEM,)),
        ],
        compiler_params=pltpu.CompilerParams(collective_id=0, has_side_effects=True),
    )(features[0], wa, wb, up)
    return gi[None], ga, jnp.transpose(gb, (0, 2, 1))


def solution(mesh):
    nd, ns = mesh.shape["dp"], mesh.shape["space"]
    cells_all = nd * 2 * ns * CELLS
    run = functools.partial(body, nd, ns, 1.0 / math.sqrt(cells_all), 1.0 / math.sqrt(cells_all / 8))
    return jax.shard_map(
        run,
        mesh=mesh,
        in_specs=(P("dp", None, "space", None), P(), P(), P("dp", None, "space", None)),
        out_specs=(P("dp", None, "space", None), P(), P(None, None, "space")),
        check_vma=False,
    )
```
